128 devices in a mesh: brick: 32 (over x, z_lo, y), scan: 4 (over z_hi, core).
Axes of the slice: x: 4, y: 4, z: 4 (z_hi: 2, z_lo: 2; z = z_hi * 2 + z_lo), core: 2. Of those that a mesh axis runs over, the one named last changes fastest.
Arguments:
- tomogram: bfloat16 [1024, 128, 128], P(('brick', 'scan')), may hold values from -6 to 6
- deformed: bfloat16 [4, 1024, 128, 128], P('scan', 'brick'), may hold values from -6 to 6
- subvoxel: float32 [4, 3, 32, 25], P('scan', None, 'brick'), may hold values from 0 to 0.99
- offsets: int32 [4, 3, 512], P('scan', None, 'brick'), may hold values from -15 to 15, as said below
Outputs:
- residual_map: bfloat16 [4, 1024, 128, 128], P('scan', 'brick')
- node_rhs: float32 [4, 3, 32, 25], P('scan', None, 'brick')
The draws below stay inside these ranges and needn't reach their ends.
Inputs may be any that keep to these rules, and one draw needn't show every extreme that they name: offsets[k, c, e] lies in -(15) .. 15 and both ends occur.
All inputs are finite; a program needn't handle non-finite values.
Results may differ from the reference program's by a relative error of at most 0.0095.
Values may be sent and summed in bfloat16 or wider, within the bound.
A program may use at most 128 MiB of HBM per device.

```python
import jax
import jax.numpy as jnp
from jax import lax

E = 32
HALO = 16
RADIUS = 3
NXY = 128
SCANS = 4
NZ = 1024
EXY = 4
NODE_Z = 32
NODES_XY = 25
ELEMS = 512


def draw_offsets(key, part):
    base = jax.random.randint(key, (SCANS, 3, ELEMS), -(HALO - 1), HALO)
    spots = jax.random.randint(jax.random.fold_in(key, 7), (2,), 0, ELEMS)
    base = base.at[0, 0, spots[0]].set(HALO - 1)
    base = base.at[SCANS - 1, 0, spots[1]].set(-(HALO - 1))
    return base.astype(jnp.int32)


def level_of(stream_key, dims, cuts, smallest, high):
    gain = 1.0
    for dim, shards_of in cuts:
        draws = jax.random.uniform(jax.random.fold_in(jax.random.fold_in(stream_key, 6), dim), (shards_of,), jnp.float32, smallest / len(cuts), high / len(cuts))
        gain = gain * jnp.repeat(jnp.exp(draws), dims[dim] // shards_of).reshape((-1,) + (1,) * (len(dims) - 1 - dim))
    return gain


def centred(own_key, dims, scale, limit, cuts=(), kind=jnp.bfloat16):
    factor_of = level_of(own_key, dims, cuts, -0.22, 0.18) if cuts else 1.0
    values = jax.random.normal(own_key, dims, jnp.float32) * scale * factor_of
    return jnp.minimum(jnp.maximum(values, -limit), limit).astype(kind)


def setup_inputs(seed: int = 0) -> dict:
    key_of = jax.random.split(jax.random.key(seed), 5)
    tomogram = centred(key_of[0], (NZ, NXY, NXY), 1.0, 6.0, ((0, 128),))
    deformed = centred(key_of[1], (SCANS, NZ, NXY, NXY), 1.0, 6.0, ((0, 4), (1, 32)))
    subvoxel = jnp.clip(0.99 * jax.random.uniform(key_of[2], (SCANS, 3, NODE_Z, NODES_XY), jnp.float32) ** level_of(key_of[2], (SCANS, 3, NODE_Z, NODES_XY), ((0, 4), (2, 32)), -0.2, 0.2), 0.0, 0.99)
    offsets = draw_offsets(jax.random.fold_in(key_of[4], 71), 0)
    return {"tomogram": tomogram, "deformed": deformed, "subvoxel": subvoxel, "offsets": offsets}


gauss_sigma = 1.0


def filter_taps():
    tap_pos = jnp.arange(-RADIUS, RADIUS + 1).astype(jnp.float32)
    gaussian = jnp.exp(-tap_pos * tap_pos / (2.0 * gauss_sigma * gauss_sigma))
    smooth_taps = gaussian / jnp.sum(gaussian)
    slope_taps = tap_pos * gaussian / jnp.sum(tap_pos * tap_pos * gaussian)
    return smooth_taps.astype(jnp.bfloat16), slope_taps.astype(jnp.bfloat16)


def band_matrix(coeff, cross_width):
    distance = jnp.arange(cross_width)[:, None] - jnp.arange(cross_width)[None, :]
    band_table = jnp.zeros((cross_width, cross_width), jnp.float32)
    for tap in range(2 * RADIUS + 1):
        band_table = band_table + jnp.where(distance == tap - RADIUS, coeff[tap].astype(jnp.float32), jnp.float32(0.0))
    return band_table.astype(jnp.bfloat16)


def z_stencil(field, coeff, planes):
    stencil_sum = jnp.zeros((planes,) + field.shape[1:], jnp.float32)
    for tap in range(2 * RADIUS + 1):
        stencil_sum = stencil_sum + coeff[tap].astype(jnp.float32) * field[tap:tap + planes].astype(jnp.float32)
    return stencil_sum.astype(jnp.bfloat16)


def gradients(extended):
    smooth_taps, slope_taps = filter_taps()
    cross_width = extended.shape[2]
    planes = extended.shape[0] - 2 * RADIUS
    along_s = band_matrix(smooth_taps, cross_width)
    along_d = band_matrix(slope_taps, cross_width)
    both_bands = jnp.concatenate([along_s, along_d], axis=1)
    x_filtered = jnp.dot(extended.reshape(-1, cross_width), both_bands, preferred_element_type=jnp.float32)
    x_filtered = x_filtered.astype(jnp.bfloat16).reshape(extended.shape[0], extended.shape[1], 2 * cross_width)
    y_smoothed = jnp.einsum('zyx,yw->zwx', x_filtered.astype(jnp.float32), along_s.astype(jnp.float32)).astype(jnp.bfloat16)
    y_slope = jnp.einsum('zyx,yw->zwx', x_filtered[:, :, :cross_width].astype(jnp.float32), along_d.astype(jnp.float32)).astype(jnp.bfloat16)
    grad_z = z_stencil(y_smoothed[:, :, :cross_width], slope_taps, planes)
    grad_y = z_stencil(y_slope, smooth_taps, planes)
    grad_x = z_stencil(y_smoothed[:, :, cross_width:], smooth_taps, planes)
    return grad_z, grad_y, grad_x


def shape_table(edge_len):
    position = (jnp.arange(edge_len).astype(jnp.float32) + 0.5) / edge_len
    return jnp.stack([1.0 - position, position], axis=1)


def layer_terms(padded, z_start, ref_layer, grad_layer, node_pair, layer_offsets):
    edge_len = ref_layer.shape[0]
    cross_width = ref_layer.shape[1]
    per_row = cross_width // edge_len
    ref_blocks = ref_layer.reshape(edge_len, per_row, edge_len, per_row, edge_len).transpose(1, 3, 0, 2, 4)
    ref_blocks = ref_blocks.reshape(per_row * per_row, edge_len, edge_len, edge_len)
    grad_blocks = grad_layer.reshape(3, edge_len, per_row, edge_len, per_row, edge_len).transpose(2, 4, 0, 1, 3, 5)
    grad_blocks = grad_blocks.reshape(per_row * per_row, 3, edge_len, edge_len, edge_len)
    picked_nodes = []
    for j in range(2):
        for k in range(2):
            picked_nodes.append(node_pair[:, :, j:j + per_row, k:k + per_row])
    corner_nodes = jnp.stack(picked_nodes, axis=2).reshape(3, 2, 2, 2, per_row, per_row)
    corner_nodes = corner_nodes.transpose(4, 5, 0, 1, 2, 3).reshape(per_row * per_row, 3, 2, 2, 2)
    element_ids = jnp.arange(per_row * per_row, dtype=jnp.int32)
    starts_z = z_start + layer_offsets[0] + HALO
    starts_y = (element_ids // per_row) * edge_len + layer_offsets[1] + HALO
    starts_x = (element_ids % per_row) * edge_len + layer_offsets[2] + HALO

    def cut_window(start_z, start_y, start_x):
        return lax.dynamic_slice(padded, (start_z, start_y, start_x), (edge_len + 1, edge_len + 1, edge_len + 1))

    windows = jax.vmap(cut_window)(starts_z, starts_y, starts_x).astype(jnp.float32)
    shapes = shape_table(edge_len)
    subvoxel_field = jnp.einsum('enijk,ai,bj,ck->enabc', corner_nodes, shapes, shapes, shapes, precision=lax.Precision.HIGHEST)
    warped = jnp.zeros((per_row * per_row, edge_len, edge_len, edge_len), jnp.float32)
    for corner_z in range(2):
        weight_z = subvoxel_field[:, 0] if corner_z else 1.0 - subvoxel_field[:, 0]
        for corner_y in range(2):
            weight_y = subvoxel_field[:, 1] if corner_y else 1.0 - subvoxel_field[:, 1]
            for corner_x in range(2):
                weight_x = subvoxel_field[:, 2] if corner_x else 1.0 - subvoxel_field[:, 2]
                sample = windows[:, corner_z:corner_z + edge_len, corner_y:corner_y + edge_len, corner_x:corner_x + edge_len]
                warped = warped + weight_z * weight_y * weight_x * sample
    misfit = warped - ref_blocks.astype(jnp.float32)
    products = grad_blocks.astype(jnp.float32) * misfit[:, None]
    element_rhs = jnp.einsum('enabc,ai,bj,ck->enijk', products, shapes, shapes, shapes, precision=lax.Precision.HIGHEST) * (1.0 / edge_len)
    misfit_layer = misfit.reshape(per_row, per_row, edge_len, edge_len, edge_len).transpose(2, 0, 3, 1, 4)
    misfit_layer = misfit_layer.reshape(edge_len, cross_width, cross_width)
    corner_sums = element_rhs.reshape(per_row, per_row, 3, 2, 2, 2)
    planes = jnp.zeros((3, 2, per_row + 1, per_row + 1), jnp.float32)
    for j in range(2):
        for k in range(2):
            placed = corner_sums[:, :, :, :, j, k].transpose(2, 3, 0, 1)
            planes = planes + jnp.pad(placed, ((0, 0), (0, 0), (j, 1 - j), (k, 1 - k)))
    return misfit_layer, planes.reshape(3, 2, (per_row + 1) * (per_row + 1))


def reference(tomogram, deformed, subvoxel, offsets):
    extended = jnp.pad(tomogram, ((RADIUS, RADIUS), (0, 0), (0, 0)))
    grad_z, grad_y, grad_x = gradients(extended)
    gradient_all = jnp.stack([grad_z, grad_y, grad_x])
    nodes_all = jnp.concatenate([subvoxel, jnp.zeros((SCANS, 3, 1, NODES_XY), jnp.float32)], axis=2)

    def one_scan(scan_items):
        volume, node_values, scan_offsets = scan_items
        padded = jnp.pad(volume, HALO)
        node_grid = node_values.reshape(3, NODE_Z + 1, EXY + 1, EXY + 1)

        def one_layer(layer_index):
            ref_layer = lax.dynamic_slice_in_dim(tomogram, layer_index * E, E, 0)
            grad_layer = lax.dynamic_slice_in_dim(gradient_all, layer_index * E, E, 1)
            node_pair = lax.dynamic_slice_in_dim(node_grid, layer_index, 2, 1)
            layer_offsets = lax.dynamic_slice_in_dim(scan_offsets, layer_index * EXY * EXY, EXY * EXY, 1)
            return layer_terms(padded, layer_index * E, ref_layer, grad_layer, node_pair, layer_offsets)

        misfits, planes = lax.map(one_layer, jnp.arange(NODE_Z, dtype=jnp.int32))
        residual_scan = misfits.reshape(NZ, NXY, NXY).astype(jnp.bfloat16)
        bottoms = planes[:, :, 0]
        tops = planes[:, :, 1]
        assembled = bottoms + jnp.concatenate([jnp.zeros_like(tops[:1]), tops[:-1]], axis=0)
        return residual_scan, assembled.transpose(1, 0, 2)

    residual_map, node_rhs = lax.map(one_scan, (deformed, nodes_all, offsets))
    return residual_map, node_rhs
```

```python
import functools

import jax
import jax.numpy as jnp
import ml_dtypes
import numpy as np
from jax import lax
from jax.experimental import pallas as pl
from jax.experimental.pallas import tpu as pltpu
from jax.sharding import PartitionSpec as P

E = 32
HALO = 16
RADIUS = 3
NXY = 128
PER_ROW = 4
NODES = 5
GAUSS_SIGMA = 1.0

WIN = 40
WPLANES = 34
VPLANES = E + 2 * HALO
YPAD = HALO
VROWS = 168
GROUP = 4


def filter_taps():
    tap_pos = np.arange(-RADIUS, RADIUS + 1).astype(np.float32)
    gaussian = np.exp(-tap_pos * tap_pos / np.float32(2.0 * GAUSS_SIGMA * GAUSS_SIGMA))
    smooth = gaussian / np.sum(gaussian)
    slope = tap_pos * gaussian / np.sum(tap_pos * tap_pos * gaussian)
    return (
        [float(v) for v in smooth.astype(ml_dtypes.bfloat16)],
        [float(v) for v in slope.astype(ml_dtypes.bfloat16)],
    )


SMOOTH, SLOPE = filter_taps()


def padded_2(cells, axis, dim, width):
    count = lax.axis_size(axis)
    ends = count - 1
    head = lax.slice_in_dim(cells, 0, width, axis=dim)
    tail = lax.slice_in_dim(cells, cells.shape[dim] - width, cells.shape[dim], axis=dim)
    return jnp.concatenate(
        [
            lax.ppermute(tail, axis, [(i, (i + 1) % count) for i in range(ends)]),
            cells,
            lax.ppermute(head, axis, [((i + 1) % count, i) for i in range(ends)]),
        ],
        axis=dim,
    )


def passed_along(block, axis, distance):
    devices = range(lax.axis_size(axis))
    route = [(i - distance, i) for i in devices if i - distance in devices]
    return lax.ppermute(block, axis, route)


def iota(shape, dim):
    return lax.broadcasted_iota(jnp.int32, shape, dim)


def band(distance, taps):
    table = jnp.zeros(distance.shape, jnp.float32)
    for tap in range(2 * RADIUS + 1):
        table = jnp.where(distance == tap - RADIUS, taps[tap], table)
    return table


def hat(shape, dim, node):
    voxel = iota(shape, dim)
    elem = voxel // E
    upper = ((voxel % E).astype(jnp.float32) + 0.5) / E
    return jnp.where(elem == node, 1.0 - upper, jnp.where(elem + 1 == node, upper, 0.0))


def filter_planes(tomo_ref, xf, grads):
    d = iota((NXY, NXY), 0) - iota((NXY, NXY), 1)
    along_x = jnp.concatenate([band(d, SMOOTH), band(d, SLOPE)], axis=1).astype(jnp.bfloat16)
    along_y = jnp.concatenate([band(-d, SMOOTH), band(-d, SLOPE)], axis=0).astype(jnp.bfloat16)
    pairs = (E + 2 * RADIUS) // 2

    def x_step(i, _):
        two = tomo_ref[pl.ds(2 * i, 2)].reshape(2 * NXY, NXY)
        out = jnp.dot(two, along_x, preferred_element_type=jnp.float32)
        xf[pl.ds(2 * i, 2)] = out.astype(jnp.bfloat16).reshape(2, NXY, 2 * NXY)
        return 0

    lax.fori_loop(0, pairs, x_step, 0)

    def y_step(i, _):
        for k in range(2):
            z = 2 * i + k
            out = jnp.dot(along_y, xf[z], preferred_element_type=jnp.float32)
            grads[0, z] = out[:NXY, :NXY]
            grads[1, z] = out[NXY:, :NXY]
            grads[2, z] = out[:NXY, NXY:]
        return 0

    lax.fori_loop(0, pairs, y_step, 0)


def spread_volume(vol_ref, volf):
    zeros_lo = jnp.zeros((YPAD, NXY), jnp.float32)
    zeros_hi = jnp.zeros((VROWS - YPAD - NXY, NXY), jnp.float32)

    def step(z, _):
        volf[z, :YPAD] = zeros_lo
        volf[z, YPAD : YPAD + NXY] = vol_ref[z].astype(jnp.float32)
        volf[z, YPAD + NXY :] = zeros_hi
        return 0

    lax.fori_loop(0, VPLANES, step, 0)


def warp_layer(offs, nodes, volf, tomo_ref, grads, lhs, win, ysum, res_ref, rhs_ref):
    ysum[...] = jnp.zeros_like(ysum)

    def element_row(ey, _):
        src = iota((NXY, NXY), 0)
        dst = iota((NXY, NXY), 1)
        blocks = []
        for ex in range(PER_ROW):
            ox = offs[2, ey * PER_ROW + ex]
            mine = dst // E == ex
            here = jnp.where(mine & (src == dst + ox), 1.0, 0.0)
            after = jnp.where(mine & (src == dst + ox + 1), 1.0, 0.0)
            blocks.append(jnp.concatenate([here, after - here], axis=1))
        shift = jnp.concatenate(blocks, axis=0).astype(jnp.bfloat16)

        def gather_planes(q, _):
            for ex in range(PER_ROW):
                oz = offs[0, ey * PER_ROW + ex] + HALO
                oy = offs[1, ey * PER_ROW + ex] + ey * E + YPAD
                two = []
                for k in range(2):
                    z = jnp.minimum(2 * q + k + oz, VPLANES - 1)
                    two.append(volf[z, pl.ds(oy, WIN), :])
                lhs[pl.ds(pl.multiple_of(q * 2 * WIN, 2 * WIN), 2 * WIN), ex * NXY : (ex + 1) * NXY] = (
                    jnp.concatenate(two, axis=0).astype(jnp.bfloat16)
                )
            return 0

        lax.fori_loop(0, WPLANES // 2, gather_planes, 0)
        rows = WPLANES * WIN
        for r0 in range(0, rows, 480):
            r1 = min(r0 + 480, rows)
            out = jnp.dot(lhs[r0:r1, :], shift, preferred_element_type=jnp.float32)
            win[0, r0:r1, :] = out[:, :NXY]
            win[1, r0:r1, :] = out[:, NXY:]

        for half in range(2):
            pb = ((iota((16, NXY), 0).astype(jnp.float32)) + (16 * half + 0.5)) / E
            start, slope = [], []
            for c in range(3):
                planes = []
                for p in range(2):
                    lo = jnp.zeros((16, NXY), jnp.float32)
                    hi = jnp.zeros((16, NXY), jnp.float32)
                    for ix in range(NODES):
                        weight = hat((16, NXY), 1, ix)
                        lo = lo + nodes(p, c, ey * NODES + ix) * weight
                        hi = hi + nodes(p, c, (ey + 1) * NODES + ix) * weight
                    planes.append(lo * (1.0 - pb) + hi * pb)
                rise = (planes[1] - planes[0]) * (1.0 / E)
                start.append(planes[0] + 0.5 * rise)
                slope.append(rise)
            yrow = pl.multiple_of(ey * E + half * 16, 16)

            def planes_step(group, carry):
                sums, prefix = list(carry[:3]), list(carry[3:])
                z0 = group * GROUP

                def corner_rows(z):
                    r = pl.multiple_of(z * WIN, 8) + 16 * half
                    return (
                        win[0, pl.ds(r, 16), :],
                        win[1, pl.ds(r, 16), :],
                        win[0, pl.ds(r + 1, 16), :],
                        win[1, pl.ds(r + 1, 16), :],
                    )

                misfits = []
                lower = corner_rows(z0)
                for k in range(GROUP):
                    z = z0 + k
                    upper = corner_rows(z + 1)
                    zf = z.astype(jnp.float32)
                    wz, wy, wx = [start[c] + zf * slope[c] for c in range(3)]

                    def in_plane(rows):
                        a = rows[0] + wx * rows[1]
                        b = rows[2] + wx * rows[3]
                        return a + wy * (b - a)

                    t0 = in_plane(lower)
                    t1 = in_plane(upper)
                    ref = tomo_ref[z + RADIUS, pl.ds(yrow, 16), :].astype(jnp.float32)
                    misfit = t0 + wz * (t1 - t0) - ref
                    res_ref[z, pl.ds(yrow, 16), :] = misfit.astype(jnp.bfloat16)
                    misfits.append(misfit)
                    lower = upper
                for c in range(3):
                    g = [grads[c, z0 + k, pl.ds(yrow, 16), :] for k in range(GROUP + 2 * RADIUS)]
                    for k in range(GROUP):
                        if c == 0:
                            grad = g[k + 4] - g[k + 2]
                            for t in (2, 3):
                                grad = grad + (SLOPE[3 + t] / SLOPE[4]) * (g[k + 3 + t] - g[k + 3 - t])
                        else:
                            grad = g[k + 3]
                            for t in (1, 2, 3):
                                grad = grad + (SMOOTH[3 + t] / SMOOTH[3]) * (g[k + 3 + t] + g[k + 3 - t])
                        sums[c] = sums[c] + grad * misfits[k]
                        prefix[c] = prefix[c] + sums[c]
                return (*sums, *prefix)

            zero = jnp.zeros((16, NXY), jnp.float32)
            done = lax.fori_loop(0, E // GROUP, planes_step, (zero,) * 6)
            for c in range(3):
                scale = (SLOPE[4] if c == 0 else SMOOTH[3]) / E
                total = done[c] * scale
                top = ((E + 0.5) * total - done[3 + c] * scale) * (1.0 / E)
                for p, part in ((0, total - top), (1, top)):
                    for j, weight in ((0, 1.0 - pb), (1, pb)):
                        row = jnp.sum(part * weight, axis=0, keepdims=True)
                        at = (p * 3 + c) * 8 + ey + j
                        ysum[pl.ds(at, 1), :] = ysum[pl.ds(at, 1), :] + row
        return 0

    lax.fori_loop(0, PER_ROW, element_row, 0)
    voxel = iota((NXY, NXY), 0)
    node = iota((NXY, NXY), 1)
    upper = ((voxel % E).astype(jnp.float32) + 0.5) / E
    to_nodes = jnp.where(voxel // E == node, 1.0 - upper, 0.0) + jnp.where(voxel // E + 1 == node, upper, 0.0)
    rhs_ref[...] = jnp.dot(
        ysum[...], to_nodes, preferred_element_type=jnp.float32, precision=lax.Precision.HIGHEST
    )


def layer_kernel(offs, lo, hi, vol_ref, tomo_ref, res_ref, rhs_ref, volf, xf, grads, lhs, win, ysum):
    filter_planes(tomo_ref, xf, grads)
    spread_volume(vol_ref, volf)

    def nodes(p, c, i):
        return (hi if p else lo)[c, i]

    warp_layer(offs, nodes, volf, tomo_ref, grads, lhs, win, ysum, res_ref, rhs_ref)


def layer(offsets, lo, hi, vol, tomo):
    smem = pl.BlockSpec(memory_space=pltpu.SMEM)
    vmem = pl.BlockSpec(memory_space=pltpu.VMEM)
    tall = E + 2 * RADIUS
    return pl.pallas_call(
        layer_kernel,
        out_shape=(
            jax.ShapeDtypeStruct((E, NXY, NXY), jnp.bfloat16),
            jax.ShapeDtypeStruct((48, NXY), jnp.float32),
        ),
        in_specs=[smem, smem, smem, vmem, vmem],
        out_specs=(vmem, vmem),
        scratch_shapes=[
            pltpu.VMEM((VPLANES, VROWS, NXY), jnp.float32),
            pltpu.VMEM((tall, NXY, 2 * NXY), jnp.bfloat16),
            pltpu.VMEM((3, tall, NXY, NXY), jnp.float32),
            pltpu.VMEM((WPLANES * WIN, PER_ROW * NXY), jnp.bfloat16),
            pltpu.VMEM((2, WPLANES * WIN, NXY), jnp.float32),
            pltpu.VMEM((48, NXY), jnp.float32),
        ],
        compiler_params=pltpu.CompilerParams(vmem_limit_bytes=48 << 20),
    )(offsets, lo, hi, vol, tomo)


def body(tomogram, deformed, subvoxel, offsets):
    ref_slab = lax.all_gather(tomogram, "scan", axis=0, tiled=True)
    extended = padded_2(ref_slab, "brick", 0, RADIUS)
    above = passed_along(subvoxel, "brick", -1)
    vol = padded_2(deformed[0], "brick", 0, HALO)
    residual, rhs = layer(offsets[0], subvoxel[0, :, 0], above[0, :, 0], vol, extended)
    rhs = rhs.reshape(2, 3, 8, NXY)[:, :, :NODES, :NODES].reshape(2, 1, 3, 1, NODES * NODES)
    node_rhs = rhs[0] + passed_along(rhs[1], "brick", 1)
    return residual[None], node_rhs


def solution(mesh):
    return jax.shard_map(
        body,
        mesh=mesh,
        in_specs=(
            P(("brick", "scan"), None, None),
            P("scan", "brick", None, None),
            P("scan", None, "brick", None),
            P("scan", None, "brick"),
        ),
        out_specs=(P("scan", "brick", None, None), P("scan", None, "brick", None)),
        check_vma=False,
    )
```

```python
import jax
import jax.numpy as jnp
import ml_dtypes
import numpy as np
from jax import lax
from jax.experimental import pallas as pl
from jax.experimental.pallas import tpu as pltpu
from jax.sharding import PartitionSpec as P

E = 32
HALO = 16
RADIUS = 3
NXY = 128
PER_ROW = 4
NODES = 5
GAUSS_SIGMA = 1.0

WIN = 40
WPLANES = 34
VPLANES = E + 2 * HALO
YPAD = HALO
VROWS = 168
GROUP = 4


def filter_taps():
    tap_pos = np.arange(-RADIUS, RADIUS + 1).astype(np.float32)
    gaussian = np.exp(-tap_pos * tap_pos / np.float32(2.0 * GAUSS_SIGMA * GAUSS_SIGMA))
    smooth = gaussian / np.sum(gaussian)
    slope = tap_pos * gaussian / np.sum(tap_pos * tap_pos * gaussian)
    return (
        [float(v) for v in smooth.astype(ml_dtypes.bfloat16)],
        [float(v) for v in slope.astype(ml_dtypes.bfloat16)],
    )


SMOOTH, SLOPE = filter_taps()


def iota(shape, dim):
    return lax.broadcasted_iota(jnp.int32, shape, dim)


def band(distance, taps):
    table = jnp.zeros(distance.shape, jnp.float32)
    for tap in range(2 * RADIUS + 1):
        table = jnp.where(distance == tap - RADIUS, taps[tap], table)
    return table


def filter_planes(tomo_ref, xf, grads):
    d = iota((NXY, NXY), 0) - iota((NXY, NXY), 1)
    along_x = jnp.concatenate([band(d, SMOOTH), band(d, SLOPE)], axis=1).astype(jnp.bfloat16)
    along_y = jnp.concatenate([band(-d, SMOOTH), band(-d, SLOPE)], axis=0).astype(jnp.bfloat16)
    pairs = (E + 2 * RADIUS) // 2

    def x_step(i, _):
        two = tomo_ref[pl.ds(2 * i, 2)].reshape(2 * NXY, NXY)
        out = jnp.dot(two, along_x, preferred_element_type=jnp.float32)
        xf[pl.ds(2 * i, 2)] = out.astype(jnp.bfloat16).reshape(2, NXY, 2 * NXY)
        return 0

    lax.fori_loop(0, pairs, x_step, 0)

    def y_step(i, _):
        for k in range(2):
            z = 2 * i + k
            out = jnp.dot(along_y, xf[z], preferred_element_type=jnp.float32)
            grads[0, z] = out[:NXY, :NXY]
            grads[1, z] = out[NXY:, :NXY]
            grads[2, z] = out[:NXY, NXY:]
        return 0

    lax.fori_loop(0, pairs, y_step, 0)


def warp_layer(offs, fields, volf, tomo_ref, grads, lhs, win, ysum, res_ref, row_done):
    ysum[...] = jnp.zeros_like(ysum)

    def element_row(ey, _):
        src = iota((NXY, NXY), 0)
        dst = iota((NXY, NXY), 1)
        blocks = []
        for ex in range(PER_ROW):
            ox = offs[2, ey * PER_ROW + ex]
            mine = dst // E == ex
            here = jnp.where(mine & (src == dst + ox), 1.0, 0.0)
            after = jnp.where(mine & (src == dst + ox + 1), 1.0, 0.0)
            blocks.append(jnp.concatenate([here, after - here], axis=1))
        shift = jnp.concatenate(blocks, axis=0).astype(jnp.bfloat16)

        def gather_planes(q, _):
            for ex in range(PER_ROW):
                oz = offs[0, ey * PER_ROW + ex] + HALO
                oy = offs[1, ey * PER_ROW + ex] + ey * E + YPAD
                two = []
                for k in range(2):
                    z = jnp.minimum(2 * q + k + oz, VPLANES - 1)
                    two.append(volf[z, pl.ds(oy, WIN), :])
                lhs[pl.ds(pl.multiple_of(q * 2 * WIN, 2 * WIN), 2 * WIN), ex * NXY : (ex + 1) * NXY] = (
                    jnp.concatenate(two, axis=0).astype(jnp.bfloat16)
                )
            return 0

        lax.fori_loop(0, WPLANES // 2, gather_planes, 0)
        rows = WPLANES * WIN
        for r0 in range(0, rows, 480):
            r1 = min(r0 + 480, rows)
            out = jnp.dot(lhs[r0:r1, :], shift, preferred_element_type=jnp.float32)
            win[0, r0:r1, :] = out[:, :NXY]
            win[1, r0:r1, :] = out[:, NXY:]

        for half in range(2):
            pb = ((iota((16, NXY), 0).astype(jnp.float32)) + (16 * half + 0.5)) / E
            start, slope = [], []
            for c in range(3):
                planes = []
                for p in range(2):
                    at = p * 8 + c
                    lo = fields[ey, at : at + 1, :]
                    hi = fields[ey + 1, at : at + 1, :]
                    planes.append(lo * (1.0 - pb) + hi * pb)
                rise = (planes[1] - planes[0]) * (1.0 / E)
                start.append(planes[0] + 0.5 * rise)
                slope.append(rise)
            yrow = pl.multiple_of(ey * E + half * 16, 16)

            def planes_step(group, carry):
                sums, prefix = list(carry[:3]), list(carry[3:])
                z0 = group * GROUP

                def corner_rows(z):
                    r = pl.multiple_of(z * WIN, 8) + 16 * half
                    return (
                        win[0, pl.ds(r, 16), :],
                        win[1, pl.ds(r, 16), :],
                        win[0, pl.ds(r + 1, 16), :],
                        win[1, pl.ds(r + 1, 16), :],
                    )

                misfits = []
                lower = corner_rows(z0)
                for k in range(GROUP):
                    z = z0 + k
                    upper = corner_rows(z + 1)
                    zf = z.astype(jnp.float32)
                    wz, wy, wx = [start[c] + zf * slope[c] for c in range(3)]

                    def in_plane(rows):
                        a = rows[0] + wx * rows[1]
                        b = rows[2] + wx * rows[3]
                        return a + wy * (b - a)

                    t0 = in_plane(lower)
                    t1 = in_plane(upper)
                    ref = tomo_ref[z + RADIUS, pl.ds(yrow, 16), :].astype(jnp.float32)
                    misfit = t0 + wz * (t1 - t0) - ref
                    res_ref[z, pl.ds(yrow, 16), :] = misfit.astype(jnp.bfloat16)
                    misfits.append(misfit)
                    lower = upper
                for c in range(3):
                    g = [grads[c, z0 + k, pl.ds(yrow, 16), :] for k in range(GROUP + 2 * RADIUS)]
                    for k in range(GROUP):
                        if c == 0:
                            grad = g[k + 4] - g[k + 2]
                            for t in (2, 3):
                                grad = grad + (SLOPE[3 + t] / SLOPE[4]) * (g[k + 3 + t] - g[k + 3 - t])
                        else:
                            grad = g[k + 3]
                            for t in (1, 2, 3):
                                grad = grad + (SMOOTH[3 + t] / SMOOTH[3]) * (g[k + 3 + t] + g[k + 3 - t])
                        sums[c] = sums[c] + grad * misfits[k]
                        prefix[c] = prefix[c] + sums[c]
                return (*sums, *prefix)

            zero = jnp.zeros((16, NXY), jnp.float32)
            done = lax.fori_loop(0, E // GROUP, planes_step, (zero,) * 6)
            for c in range(3):
                scale = (SLOPE[4] if c == 0 else SMOOTH[3]) / E
                total = done[c] * scale
                top = ((E + 0.5) * total - done[3 + c] * scale) * (1.0 / E)
                for p, part in ((0, total - top), (1, top)):
                    for j, weight in ((0, 1.0 - pb), (1, pb)):
                        row = jnp.sum(part * weight, axis=0, keepdims=True)
                        at = p * 8 + c
                        ysum[ey + j, at : at + 1, :] = ysum[ey + j, at : at + 1, :] + row
        row_done(ey)
        return 0

    lax.fori_loop(0, PER_ROW, element_row, 0)


def node_lanes(iy):
    node = iota((NXY, NXY), 1) - NODES * iy
    voxel = iota((NXY, NXY), 0)
    upper = ((voxel % E).astype(jnp.float32) + 0.5) / E
    weight = jnp.where(voxel // E == node, 1.0 - upper, 0.0) + jnp.where(voxel // E + 1 == node, upper, 0.0)
    return jnp.where(node < NODES, weight, 0.0)


def node_fields(nodes, fields):
    for iy in range(NODES):
        fields[iy] = lax.dot_general(
            nodes[...],
            node_lanes(iy),
            (((1,), (1,)), ((), ())),
            preferred_element_type=jnp.float32,
            precision=lax.Precision.HIGHEST,
        )


def node_sums(ysum):
    total = jnp.zeros((16, NXY), jnp.float32)
    for iy in range(NODES):
        total = total + jnp.dot(
            ysum[iy], node_lanes(iy), preferred_element_type=jnp.float32, precision=lax.Precision.HIGHEST
        )
    return total


UP, DOWN, SIBLING, OTHER, RELAY, LOW_A, LOW_B, LOW_RELAY, HIGH_A, HIGH_B, HIGH_RELAY, NODE, TAIL = range(13)


def step_kernel(
    offs, sub_ref, tomo_hbm, vol_hbm, res_hbm, rhs_ref,
    own, halo, tomo, volf, xf, grads, lhs, win, ysum, fields, nodes, above, res, sums, tail,
    send, recv, local,
):
    bricks = lax.axis_size("brick")
    b = lax.axis_index("brick")
    s = lax.axis_index("scan")
    block = tomo_hbm.shape[0]
    has_above = b < bricks - 1
    has_below = b > 0
    odd = lax.rem(s, 2) == 1
    sibling = s + 1 - 2 * lax.rem(s, 2)
    other = lax.rem(s + 2, 4)

    def remote(kind, src, dst, brick, scan):
        return pltpu.make_async_remote_copy(
            src_ref=src,
            dst_ref=dst,
            send_sem=send.at[kind],
            recv_sem=recv.at[kind],
            device_id={"brick": brick, "scan": scan},
            device_id_type=pl.DeviceIdType.MESH,
        )

    def block_at(i):
        return tomo.at[pl.ds(RADIUS + block * i, block)]

    low_edge = tomo.at[pl.ds(0, RADIUS)]
    high_edge = tomo.at[pl.ds(RADIUS + E, RADIUS)]
    up = remote(UP, vol_hbm.at[0, pl.ds(E - HALO, HALO)], halo.at[0], b + 1, s)
    down = remote(DOWN, vol_hbm.at[0, pl.ds(0, HALO)], halo.at[1], b - 1, s)
    to_sibling = remote(SIBLING, tomo_hbm, block_at(s), b, sibling)
    to_other = remote(OTHER, tomo_hbm, block_at(s), b, other)
    relay = remote(RELAY, block_at(other), block_at(other), b, sibling)
    from_relay = remote(RELAY, block_at(lax.rem(sibling + 2, 4)), block_at(lax.rem(sibling + 2, 4)), b, sibling)
    from_sibling = remote(SIBLING, tomo_hbm, block_at(sibling), b, sibling)
    from_other = remote(OTHER, tomo_hbm, block_at(other), b, other)
    last_planes = tomo_hbm.at[pl.ds(block - RADIUS, RADIUS)]
    first_planes = tomo_hbm.at[pl.ds(0, RADIUS)]
    low_a = remote(LOW_A, last_planes, low_edge, b + 1, 3)
    low_b = remote(LOW_B, last_planes, low_edge, b + 1, 1)
    low_relay = remote(LOW_RELAY, low_edge, low_edge, b, sibling)
    high_a = remote(HIGH_A, first_planes, high_edge, b - 1, 0)
    high_b = remote(HIGH_B, first_planes, high_edge, b - 1, 2)
    high_relay = remote(HIGH_RELAY, high_edge, high_edge, b, sibling)
    node = remote(NODE, sub_ref, above, b - 1, s)

    get_own = pltpu.make_async_copy(vol_hbm.at[0], own, local.at[0])
    get_tomo = pltpu.make_async_copy(tomo_hbm, block_at(s), local.at[1])
    get_own.start()
    get_tomo.start()

    barrier = pltpu.get_barrier_semaphore()

    def greet(brick, scan):
        pl.semaphore_signal(
            barrier, inc=1, device_id={"brick": brick, "scan": scan}, device_id_type=pl.DeviceIdType.MESH
        )

    greet(b, sibling)
    greet(b, other)

    @pl.when(has_above)
    def _():
        greet(b + 1, s)

        @pl.when(s == 3)
        def _():
            greet(b + 1, 1)

        @pl.when(s == 2)
        def _():
            greet(b + 1, 0)

    @pl.when(has_below)
    def _():
        greet(b - 1, s)

        @pl.when(s == 1)
        def _():
            greet(b - 1, 3)

        @pl.when(s == 0)
        def _():
            greet(b - 1, 2)

    from_above = jnp.where(has_above, jnp.where(s >= 2, 2, 1), 0)
    from_below = jnp.where(has_below, jnp.where(s <= 1, 2, 1), 0)
    pl.semaphore_wait(barrier, 2 + from_above + from_below)

    to_other.start()
    to_sibling.start()

    @pl.when(has_above & (s == 3))
    def _():
        low_a.start()
        low_b.start()

    @pl.when(has_below & (s == 0))
    def _():
        high_a.start()
        high_b.start()

    @pl.when(has_above)
    def _():
        up.start()

    @pl.when(has_below)
    def _():
        down.start()
        node.start()

    zeros_lo = jnp.zeros((YPAD, NXY), jnp.float32)
    zeros_hi = jnp.zeros((VROWS - YPAD - NXY, NXY), jnp.float32)

    def borders(z, _):
        volf[z, :YPAD] = zeros_lo
        volf[z, YPAD + NXY :] = zeros_hi
        return 0

    lax.fori_loop(0, VPLANES, borders, 0)
    nodes[...] = jnp.zeros_like(nodes)
    for c in range(3):
        nodes[c : c + 1, : NODES * NODES] = sub_ref[0, c]

    @pl.when(jnp.logical_not(has_below))
    def _():
        halo[0] = jnp.zeros((HALO, NXY, NXY), jnp.bfloat16)
        tomo[:RADIUS] = jnp.zeros((RADIUS, NXY, NXY), jnp.bfloat16)

    @pl.when(jnp.logical_not(has_above))
    def _():
        halo[1] = jnp.zeros((HALO, NXY, NXY), jnp.bfloat16)
        tomo[RADIUS + E :] = jnp.zeros((RADIUS, NXY, NXY), jnp.bfloat16)

    get_own.wait()

    def spread_own(z, _):
        volf[HALO + z, YPAD : YPAD + NXY] = own[z].astype(jnp.float32)
        return 0

    lax.fori_loop(0, E, spread_own, 0)

    from_other.wait_recv()
    relay.start()

    @pl.when(has_below & odd)
    def _():
        @pl.when(s == 3)
        def _():
            low_a.wait_recv()

        @pl.when(s == 1)
        def _():
            low_b.wait_recv()

        low_relay.start()

    @pl.when(has_above & jnp.logical_not(odd))
    def _():
        @pl.when(s == 0)
        def _():
            high_a.wait_recv()

        @pl.when(s == 2)
        def _():
            high_b.wait_recv()

        high_relay.start()

    get_tomo.wait()
    from_sibling.wait_recv()
    from_relay.wait_recv()

    @pl.when(has_below & jnp.logical_not(odd))
    def _():
        low_relay.wait_recv()

    @pl.when(has_above & odd)
    def _():
        high_relay.wait_recv()

    filter_planes(tomo, xf, grads)

    @pl.when(has_above)
    def _():
        node.wait_recv()
        for c in range(3):
            nodes[8 + c : 9 + c, : NODES * NODES] = above[0, c]
        down.wait_recv()

    @pl.when(has_below)
    def _():
        up.wait_recv()

    node_fields(nodes, fields)

    def spread_halo(z, _):
        volf[z, YPAD : YPAD + NXY] = halo[0, z].astype(jnp.float32)
        volf[HALO + E + z, YPAD : YPAD + NXY] = halo[1, z].astype(jnp.float32)
        return 0

    lax.fori_loop(0, HALO, spread_halo, 0)

    def put_row(ey):
        rows = pl.ds(pl.multiple_of(ey * E, E), E)
        return pltpu.make_async_copy(res.at[:, rows], res_hbm.at[:, rows], local.at[2 + ey])

    warp_layer(offs, fields, volf, tomo, grads, lhs, win, ysum, res, lambda ey: put_row(ey).start())
    sums[...] = node_sums(ysum)
    to_above = remote(TAIL, sums.at[pl.ds(8, 8)], tail, b + 1, s)

    @pl.when(has_above)
    def _():
        to_above.start()

    to_other.wait_send()
    to_sibling.wait_send()
    relay.wait_send()

    @pl.when(has_above & (s == 3))
    def _():
        low_a.wait_send()
        low_b.wait_send()

    @pl.when(has_below & (s == 0))
    def _():
        high_a.wait_send()
        high_b.wait_send()

    @pl.when(has_below & odd)
    def _():
        low_relay.wait_send()

    @pl.when(has_above & jnp.logical_not(odd))
    def _():
        high_relay.wait_send()

    @pl.when(has_above)
    def _():
        up.wait_send()

    @pl.when(has_below)
    def _():
        down.wait_send()
        node.wait_send()

    for ey in range(PER_ROW):
        put_row(ey).wait()

    @pl.when(jnp.logical_not(has_below))
    def _():
        tail[...] = jnp.zeros_like(tail)

    @pl.when(has_below)
    def _():
        to_above.wait_recv()

    final = sums[:8] + tail[...]
    for c in range(3):
        rhs_ref[0, c] = final[c : c + 1, : NODES * NODES]

    @pl.when(has_above)
    def _():
        to_above.wait_send()


def body(tomogram, deformed, subvoxel, offsets):
    tall = E + 2 * RADIUS
    smem = pl.BlockSpec(memory_space=pltpu.SMEM)
    vmem = pl.BlockSpec(memory_space=pltpu.VMEM)
    hbm = pl.BlockSpec(memory_space=pl.ANY)
    residual, node_rhs = pl.pallas_call(
        step_kernel,
        out_shape=(
            jax.ShapeDtypeStruct((E, NXY, NXY), jnp.bfloat16),
            jax.ShapeDtypeStruct(subvoxel.shape, jnp.float32),
        ),
        in_specs=[smem, vmem, hbm, hbm],
        out_specs=(hbm, vmem),
        scratch_shapes=[
            pltpu.VMEM((E, NXY, NXY), jnp.bfloat16),
            pltpu.VMEM((2, HALO, NXY, NXY), jnp.bfloat16),
            pltpu.VMEM((tall, NXY, NXY), jnp.bfloat16),
            pltpu.VMEM((VPLANES, VROWS, NXY), jnp.float32),
            pltpu.VMEM((tall, NXY, 2 * NXY), jnp.bfloat16),
            pltpu.VMEM((3, tall, NXY, NXY), jnp.float32),
            pltpu.VMEM((WPLANES * WIN, PER_ROW * NXY), jnp.bfloat16),
            pltpu.VMEM((2, WPLANES * WIN, NXY), jnp.float32),
            pltpu.VMEM((NODES, 16, NXY), jnp.float32),
            pltpu.VMEM((NODES, 16, NXY), jnp.float32),
            pltpu.VMEM((16, NXY), jnp.float32),
            pltpu.VMEM(subvoxel.shape, jnp.float32),
            pltpu.VMEM((E, NXY, NXY), jnp.bfloat16),
            pltpu.VMEM((16, NXY), jnp.float32),
            pltpu.VMEM((8, NXY), jnp.float32),
            pltpu.SemaphoreType.DMA((13,)),
            pltpu.SemaphoreType.DMA((13,)),
            pltpu.SemaphoreType.DMA((2 + PER_ROW,)),
        ],
        compiler_params=pltpu.CompilerParams(
            collective_id=0, has_side_effects=True, vmem_limit_bytes=48 << 20
        ),
    )(offsets[0], subvoxel, tomogram, deformed)
    return residual[None], node_rhs


def solution(mesh):
    return jax.shard_map(
        body,
        mesh=mesh,
        in_specs=(
            P(("brick", "scan"), None, None),
            P("scan", "brick", None, None),
            P("scan", None, "brick", None),
            P("scan", None, "brick"),
        ),
        out_specs=(P("scan", "brick", None, None), P("scan", None, "brick", None)),
        check_vma=False,
    )
```

```python
import jax
import jax.numpy as jnp
import ml_dtypes
import numpy as np
from jax import lax
from jax.experimental import pallas as pl
from jax.experimental.pallas import tpu as pltpu
from jax.sharding import PartitionSpec as P

E = 32
HALO = 16
RADIUS = 3
NXY = 128
PER_ROW = 4
NODES = 5
GAUSS_SIGMA = 1.0

WIN = 40
WPLANES = 34
VPLANES = E + 2 * HALO
YPAD = HALO
VROWS = 168
GROUP = 4


def filter_taps():
    tap_pos = np.arange(-RADIUS, RADIUS + 1).astype(np.float32)
    gaussian = np.exp(-tap_pos * tap_pos / np.float32(2.0 * GAUSS_SIGMA * GAUSS_SIGMA))
    smooth = gaussian / np.sum(gaussian)
    slope = tap_pos * gaussian / np.sum(tap_pos * tap_pos * gaussian)
    return (
        [float(v) for v in smooth.astype(ml_dtypes.bfloat16)],
        [float(v) for v in slope.astype(ml_dtypes.bfloat16)],
    )


SMOOTH, SLOPE = filter_taps()


def iota(shape, dim):
    return lax.broadcasted_iota(jnp.int32, shape, dim)


def band(distance, taps):
    table = jnp.zeros(distance.shape, jnp.float32)
    for tap in range(2 * RADIUS + 1):
        table = jnp.where(distance == tap - RADIUS, taps[tap], table)
    return table


def write_bands(band_x, band_y):
    d = iota((NXY, NXY), 0) - iota((NXY, NXY), 1)
    band_x[...] = jnp.concatenate([band(d, SMOOTH), band(d, SLOPE)], axis=1).astype(jnp.bfloat16)
    band_y[...] = jnp.concatenate([band(-d, SMOOTH), band(-d, SLOPE)], axis=0).astype(jnp.bfloat16)


def filter_planes(band_x, band_y, tomo, grads, start, count):
    planes = tomo[pl.ds(start, count)].reshape(count * NXY, NXY)
    along_x = jnp.dot(planes, band_x[...], preferred_element_type=jnp.float32).astype(jnp.bfloat16)
    for k in range(count):
        out = jnp.dot(
            band_y[...], along_x[k * NXY : (k + 1) * NXY], preferred_element_type=jnp.float32
        )
        grads[0, start + k] = out[:NXY, :NXY]
        grads[1, start + k] = out[NXY:, :NXY]
        grads[2, start + k] = out[:NXY, NXY:]


def write_shifts(offs, shifts):
    def element_row(ey, _):
        src = iota((NXY, NXY), 0)
        dst = iota((NXY, NXY), 1)
        for ex in range(PER_ROW):
            ox = offs[2, 0, ey * PER_ROW + ex]
            mine = dst // E == ex
            here = jnp.where(mine & (src == dst + ox), 1.0, 0.0)
            after = jnp.where(mine & (src == dst + ox + 1), 1.0, 0.0)
            shifts[ey, ex * NXY : (ex + 1) * NXY, :] = jnp.concatenate(
                [here, after - here], axis=1
            ).astype(jnp.bfloat16)
        return 0

    lax.fori_loop(0, PER_ROW, element_row, 0)


def warp_layer(offs, shifts, fields, volf, tomo_ref, grads, lhs, win, ysum, res_ref, row_done):
    ysum[...] = jnp.zeros_like(ysum)

    def element_row(ey, _):
        def gather_planes(q, _):
            for ex in range(PER_ROW):
                oz = offs[0, 0, ey * PER_ROW + ex] + HALO
                oy = offs[1, 0, ey * PER_ROW + ex] + ey * E + YPAD
                two = []
                for k in range(2):
                    z = jnp.minimum(2 * q + k + oz, VPLANES - 1)
                    two.append(volf[z, pl.ds(oy, WIN), :])
                lhs[pl.ds(pl.multiple_of(q * 2 * WIN, 2 * WIN), 2 * WIN), ex * NXY : (ex + 1) * NXY] = (
                    jnp.concatenate(two, axis=0).astype(jnp.bfloat16)
                )
            return 0

        lax.fori_loop(0, WPLANES // 2, gather_planes, 0)
        rows = WPLANES * WIN
        for r0 in range(0, rows, 480):
            r1 = min(r0 + 480, rows)
            out = jnp.dot(lhs[r0:r1, :], shifts[ey], preferred_element_type=jnp.float32)
            win[0, r0:r1, :] = out[:, :NXY]
            win[1, r0:r1, :] = out[:, NXY:]

        for half in range(2):
            pb = ((iota((16, NXY), 0).astype(jnp.float32)) + (16 * half + 0.5)) / E
            start, slope = [], []
            for c in range(3):
                planes = []
                for p in range(2):
                    at = p * 8 + c
                    lo = fields[ey, at : at + 1, :]
                    hi = fields[ey + 1, at : at + 1, :]
                    planes.append(lo * (1.0 - pb) + hi * pb)
                rise = (planes[1] - planes[0]) * (1.0 / E)
                start.append(planes[0] + 0.5 * rise)
                slope.append(rise)
            yrow = pl.multiple_of(ey * E + half * 16, 16)

            def planes_step(group, carry):
                sums, prefix = list(carry[:3]), list(carry[3:])
                z0 = group * GROUP

                def corner_rows(z):
                    r = pl.multiple_of(z * WIN, 8) + 16 * half
                    return (
                        win[0, pl.ds(r, 16), :],
                        win[1, pl.ds(r, 16), :],
                        win[0, pl.ds(r + 1, 16), :],
                        win[1, pl.ds(r + 1, 16), :],
                    )

                misfits = []
                lower = corner_rows(z0)
                for k in range(GROUP):
                    z = z0 + k
                    upper = corner_rows(z + 1)
                    zf = z.astype(jnp.float32)
                    wz, wy, wx = [start[c] + zf * slope[c] for c in range(3)]

                    def in_plane(rows):
                        a = rows[0] + wx * rows[1]
                        b = rows[2] + wx * rows[3]
                        return a + wy * (b - a)

                    t0 = in_plane(lower)
                    t1 = in_plane(upper)
                    ref = tomo_ref[z + RADIUS, pl.ds(yrow, 16), :].astype(jnp.float32)
                    misfit = t0 + wz * (t1 - t0) - ref
                    res_ref[z, pl.ds(yrow, 16), :] = misfit.astype(jnp.bfloat16)
                    misfits.append(misfit)
                    lower = upper
                for c in range(3):
                    g = [grads[c, z0 + k, pl.ds(yrow, 16), :] for k in range(GROUP + 2 * RADIUS)]
                    for k in range(GROUP):
                        if c == 0:
                            grad = g[k + 4] - g[k + 2]
                            for t in (2, 3):
                                grad = grad + (SLOPE[3 + t] / SLOPE[4]) * (g[k + 3 + t] - g[k + 3 - t])
                        else:
                            grad = g[k + 3]
                            for t in (1, 2, 3):
                                grad = grad + (SMOOTH[3 + t] / SMOOTH[3]) * (g[k + 3 + t] + g[k + 3 - t])
                        sums[c] = sums[c] + grad * misfits[k]
                        prefix[c] = prefix[c] + sums[c]
                return (*sums, *prefix)

            zero = jnp.zeros((16, NXY), jnp.float32)
            done = lax.fori_loop(0, E // GROUP, planes_step, (zero,) * 6)
            for c in range(3):
                scale = (SLOPE[4] if c == 0 else SMOOTH[3]) / E
                total = done[c] * scale
                top = ((E + 0.5) * total - done[3 + c] * scale) * (1.0 / E)
                for p, part in ((0, total - top), (1, top)):
                    for j, weight in ((0, 1.0 - pb), (1, pb)):
                        row = jnp.sum(part * weight, axis=0, keepdims=True)
                        at = p * 8 + c
                        ysum[ey + j, at : at + 1, :] = ysum[ey + j, at : at + 1, :] + row
        row_done(ey)
        return 0

    lax.fori_loop(0, PER_ROW, element_row, 0)


def node_lanes(iy):
    node = iota((NXY, NXY), 1) - NODES * iy
    voxel = iota((NXY, NXY), 0)
    upper = ((voxel % E).astype(jnp.float32) + 0.5) / E
    weight = jnp.where(voxel // E == node, 1.0 - upper, 0.0) + jnp.where(voxel // E + 1 == node, upper, 0.0)
    return jnp.where(node < NODES, weight, 0.0)


def node_fields(nodes, fields):
    for iy in range(NODES):
        fields[iy] = lax.dot_general(
            nodes[...],
            node_lanes(iy),
            (((1,), (1,)), ((), ())),
            preferred_element_type=jnp.float32,
            precision=lax.Precision.HIGHEST,
        )


def node_sums(ysum):
    total = jnp.zeros((16, NXY), jnp.float32)
    for iy in range(NODES):
        total = total + jnp.dot(
            ysum[iy], node_lanes(iy), preferred_element_type=jnp.float32, precision=lax.Precision.HIGHEST
        )
    return total


UP, DOWN, SIBLING, OTHER, RELAY, LOW_A, LOW_B, LOW_RELAY, HIGH_A, HIGH_B, HIGH_RELAY, NODE, TAIL = range(13)


def step_kernel(
    offs, sub_hbm, tomo_hbm, vol_hbm, res_hbm, rhs_ref,
    own, halo, tomo, res, volf, band_x, band_y, shifts, grads, lhs, win, ysum, fields, nodes, mine, above, sums, tail,
    send, recv, local,
):
    bricks = lax.axis_size("brick")
    b = lax.axis_index("brick")
    s = lax.axis_index("scan")
    block = tomo_hbm.shape[0]
    has_above = b < bricks - 1
    has_below = b > 0
    odd = lax.rem(s, 2) == 1
    sibling = s + 1 - 2 * lax.rem(s, 2)
    other = lax.rem(s + 2, 4)

    def remote(kind, src, dst, brick, scan):
        return pltpu.make_async_remote_copy(
            src_ref=src,
            dst_ref=dst,
            send_sem=send.at[kind],
            recv_sem=recv.at[kind],
            device_id={"brick": brick, "scan": scan},
            device_id_type=pl.DeviceIdType.MESH,
        )

    def block_at(i):
        return tomo.at[pl.ds(RADIUS + block * i, block)]

    low_edge = tomo.at[pl.ds(0, RADIUS)]
    high_edge = tomo.at[pl.ds(RADIUS + E, RADIUS)]
    up = remote(UP, vol_hbm.at[0, pl.ds(E - HALO + 1, HALO - 1)], halo.at[0, pl.ds(1, HALO - 1)], b + 1, s)
    down = remote(DOWN, vol_hbm.at[0, pl.ds(0, HALO)], halo.at[1], b - 1, s)
    to_sibling = remote(SIBLING, tomo_hbm, block_at(s), b, sibling)
    to_other = remote(OTHER, tomo_hbm, block_at(s), b, other)
    relay = remote(RELAY, block_at(other), block_at(other), b, sibling)
    from_relay = remote(RELAY, block_at(lax.rem(sibling + 2, 4)), block_at(lax.rem(sibling + 2, 4)), b, sibling)
    from_sibling = remote(SIBLING, tomo_hbm, block_at(sibling), b, sibling)
    from_other = remote(OTHER, tomo_hbm, block_at(other), b, other)
    last_planes = tomo_hbm.at[pl.ds(block - RADIUS, RADIUS)]
    first_planes = tomo_hbm.at[pl.ds(0, RADIUS)]
    low_a = remote(LOW_A, last_planes, low_edge, b + 1, 3)
    low_b = remote(LOW_B, tomo.at[pl.ds(E, RADIUS)], low_edge, b + 1, 1)
    low_relay = remote(LOW_RELAY, low_edge, low_edge, b, sibling)
    high_a = remote(HIGH_A, first_planes, high_edge, b - 1, 0)
    high_b = remote(HIGH_B, tomo.at[pl.ds(RADIUS, RADIUS)], high_edge, b - 1, 2)
    high_relay = remote(HIGH_RELAY, high_edge, high_edge, b, sibling)
    node = remote(NODE, sub_hbm, above, b - 1, s)

    get_own = pltpu.make_async_copy(vol_hbm.at[0], own, local.at[0])
    get_tomo = pltpu.make_async_copy(tomo_hbm, block_at(s), local.at[1])
    get_sub = pltpu.make_async_copy(sub_hbm, mine, local.at[2])
    get_own.start()
    get_tomo.start()
    get_sub.start()

    barrier = pltpu.get_barrier_semaphore()

    def greet(brick, scan):
        pl.semaphore_signal(
            barrier, inc=1, device_id={"brick": brick, "scan": scan}, device_id_type=pl.DeviceIdType.MESH
        )

    greet(b, sibling)
    greet(b, other)

    @pl.when(has_above)
    def _():
        greet(b + 1, s)

    @pl.when(has_below)
    def _():
        greet(b - 1, s)

    pl.semaphore_wait(barrier, 2 + has_above.astype(jnp.int32) + has_below.astype(jnp.int32))

    to_other.start()
    to_sibling.start()

    @pl.when(has_above & (s == 3))
    def _():
        low_a.start()

    @pl.when(has_below & (s == 0))
    def _():
        high_a.start()

    @pl.when(has_below)
    def _():
        node.start()
        down.start()

    @pl.when(has_above)
    def _():
        up.start()

    zeros_lo = jnp.zeros((YPAD, NXY), jnp.float32)
    zeros_hi = jnp.zeros((VROWS - YPAD - NXY, NXY), jnp.float32)

    def borders(z, _):
        volf[z, :YPAD] = zeros_lo
        volf[z, YPAD + NXY :] = zeros_hi
        return 0

    lax.fori_loop(0, VPLANES, borders, 0)
    nodes[...] = jnp.zeros_like(nodes)
    halo[0, 0] = jnp.zeros((NXY, NXY), jnp.bfloat16)
    get_sub.wait()
    for c in range(3):
        nodes[c : c + 1, : NODES * NODES] = mine[0, c]

    @pl.when(jnp.logical_not(has_below))
    def _():
        halo[0] = jnp.zeros((HALO, NXY, NXY), jnp.bfloat16)
        tomo[:RADIUS] = jnp.zeros((RADIUS, NXY, NXY), jnp.bfloat16)

    @pl.when(jnp.logical_not(has_above))
    def _():
        halo[1] = jnp.zeros((HALO, NXY, NXY), jnp.bfloat16)
        tomo[RADIUS + E :] = jnp.zeros((RADIUS, NXY, NXY), jnp.bfloat16)

    get_own.wait()

    def spread_own(z, _):
        volf[HALO + z, YPAD : YPAD + NXY] = own[z].astype(jnp.float32)
        return 0

    lax.fori_loop(0, E, spread_own, 0)

    def filter_block(i):
        filter_planes(band_x, band_y, tomo, grads, RADIUS + block * i, block)

    write_bands(band_x, band_y)
    get_tomo.wait()
    filter_block(s)

    from_other.wait_recv()
    relay.start()

    @pl.when(has_above & (s == 1))
    def _():
        low_b.start()

    @pl.when(has_below & (s == 2))
    def _():
        high_b.start()

    filter_block(other)
    from_sibling.wait_recv()
    filter_block(sibling)

    @pl.when(has_below & odd)
    def _():
        @pl.when(s == 3)
        def _():
            low_a.wait_recv()

        @pl.when(s == 1)
        def _():
            low_b.wait_recv()

        low_relay.start()

    @pl.when(has_above & jnp.logical_not(odd))
    def _():
        @pl.when(s == 0)
        def _():
            high_a.wait_recv()

        @pl.when(s == 2)
        def _():
            high_b.wait_recv()

        high_relay.start()

    write_shifts(offs, shifts)

    @pl.when(has_above)
    def _():
        node.wait_recv()
        for c in range(3):
            nodes[8 + c : 9 + c, : NODES * NODES] = above[0, c]

    node_fields(nodes, fields)
    from_relay.wait_recv()
    filter_block(lax.rem(sibling + 2, 4))

    @pl.when(has_below & jnp.logical_not(odd))
    def _():
        low_relay.wait_recv()

    @pl.when(has_above & odd)
    def _():
        high_relay.wait_recv()

    filter_planes(band_x, band_y, tomo, grads, 0, RADIUS)
    filter_planes(band_x, band_y, tomo, grads, RADIUS + E, RADIUS)

    @pl.when(has_above)
    def _():
        down.wait_recv()

    @pl.when(has_below)
    def _():
        up.wait_recv()

    def spread_halo(z, _):
        volf[z, YPAD : YPAD + NXY] = halo[0, z].astype(jnp.float32)
        volf[HALO + E + z, YPAD : YPAD + NXY] = halo[1, z].astype(jnp.float32)
        return 0

    lax.fori_loop(0, HALO, spread_halo, 0)

    def put_row(ey):
        rows = pl.ds(pl.multiple_of(ey * E, E), E)
        return pltpu.make_async_copy(res.at[:, rows], res_hbm.at[:, rows], local.at[3 + ey])

    warp_layer(
        offs, shifts, fields, volf, tomo, grads, lhs, win, ysum, res, lambda ey: put_row(ey).start()
    )
    sums[...] = node_sums(ysum)
    to_above = remote(TAIL, sums.at[pl.ds(8, 8)], tail, b + 1, s)

    @pl.when(has_above)
    def _():
        to_above.start()

    to_other.wait_send()
    to_sibling.wait_send()
    relay.wait_send()

    @pl.when(has_above & (s == 3))
    def _():
        low_a.wait_send()

    @pl.when(has_above & (s == 1))
    def _():
        low_b.wait_send()

    @pl.when(has_below & (s == 0))
    def _():
        high_a.wait_send()

    @pl.when(has_below & (s == 2))
    def _():
        high_b.wait_send()

    @pl.when(has_below & odd)
    def _():
        low_relay.wait_send()

    @pl.when(has_above & jnp.logical_not(odd))
    def _():
        high_relay.wait_send()

    @pl.when(has_above)
    def _():
        up.wait_send()

    @pl.when(has_below)
    def _():
        down.wait_send()
        node.wait_send()

    for ey in range(PER_ROW):
        put_row(ey).wait()

    @pl.when(jnp.logical_not(has_below))
    def _():
        tail[...] = jnp.zeros_like(tail)

    @pl.when(has_below)
    def _():
        to_above.wait_recv()

    final = sums[:8] + tail[...]
    for c in range(3):
        rhs_ref[0, c] = final[c : c + 1, : NODES * NODES]

    @pl.when(has_above)
    def _():
        to_above.wait_send()


def body(tomogram, deformed, subvoxel, offsets):
    tall = E + 2 * RADIUS
    smem = pl.BlockSpec(memory_space=pltpu.SMEM)
    vmem = pl.BlockSpec(memory_space=pltpu.VMEM)
    hbm = pl.BlockSpec(memory_space=pltpu.HBM)
    residual, node_rhs = pl.pallas_call(
        step_kernel,
        out_shape=(
            jax.ShapeDtypeStruct((E, NXY, NXY), jnp.bfloat16),
            jax.ShapeDtypeStruct(subvoxel.shape, jnp.float32),
        ),
        in_specs=[smem, hbm, hbm, hbm],
        out_specs=(hbm, vmem),
        scratch_shapes=[
            pltpu.VMEM((E, NXY, NXY), jnp.bfloat16),
            pltpu.VMEM((2, HALO, NXY, NXY), jnp.bfloat16),
            pltpu.VMEM((tall, NXY, NXY), jnp.bfloat16),
            pltpu.VMEM((E, NXY, NXY), jnp.bfloat16),
            pltpu.VMEM((VPLANES, VROWS, NXY), jnp.float32),
            pltpu.VMEM((NXY, 2 * NXY), jnp.bfloat16),
            pltpu.VMEM((2 * NXY, NXY), jnp.bfloat16),
            pltpu.VMEM((PER_ROW, PER_ROW * NXY, 2 * NXY), jnp.bfloat16),
            pltpu.VMEM((3, tall, NXY, NXY), jnp.float32),
            pltpu.VMEM((WPLANES * WIN, PER_ROW * NXY), jnp.bfloat16),
            pltpu.VMEM((2, WPLANES * WIN, NXY), jnp.float32),
            pltpu.VMEM((NODES, 16, NXY), jnp.float32),
            pltpu.VMEM((NODES, 16, NXY), jnp.float32),
            pltpu.VMEM((16, NXY), jnp.float32),
            pltpu.VMEM(subvoxel.shape, jnp.float32),
            pltpu.VMEM(subvoxel.shape, jnp.float32),
            pltpu.VMEM((16, NXY), jnp.float32),
            pltpu.VMEM((8, NXY), jnp.float32),
            pltpu.SemaphoreType.DMA((13,)),
            pltpu.SemaphoreType.DMA((13,)),
            pltpu.SemaphoreType.DMA((3 + PER_ROW,)),
        ],
        compiler_params=pltpu.CompilerParams(
            collective_id=0, has_side_effects=True, vmem_limit_bytes=60 << 20
        ),
    )(offsets.transpose(1, 0, 2), subvoxel, tomogram, deformed)
    return residual[None], node_rhs


def solution(mesh):
    return jax.shard_map(
        body,
        mesh=mesh,
        in_specs=(
            P(("brick", "scan"), None, None),
            P("scan", "brick", None, None),
            P("scan", None, "brick", None),
            P("scan", None, "brick"),
        ),
        out_specs=(P("scan", "brick", None, None), P("scan", None, "brick", None)),
        check_vma=False,
    )
```

```python
import jax
import jax.numpy as jnp
import ml_dtypes
import numpy as np
from jax import lax
from jax.experimental import pallas as pl
from jax.experimental.pallas import tpu as pltpu
from jax.sharding import PartitionSpec as P

E = 32
HALO = 16
RADIUS = 3
NXY = 128
PER_ROW = 4
NODES = 5
GAUSS_SIGMA = 1.0

WIN = 40
WPLANES = 34
VPLANES = E + 2 * HALO
YPAD = HALO
VROWS = 168
GROUP = 4


def filter_taps():
    tap_pos = np.arange(-RADIUS, RADIUS + 1).astype(np.float32)
    gaussian = np.exp(-tap_pos * tap_pos / np.float32(2.0 * GAUSS_SIGMA * GAUSS_SIGMA))
    smooth = gaussian / np.sum(gaussian)
    slope = tap_pos * gaussian / np.sum(tap_pos * tap_pos * gaussian)
    return (
        [float(v) for v in smooth.astype(ml_dtypes.bfloat16)],
        [float(v) for v in slope.astype(ml_dtypes.bfloat16)],
    )


SMOOTH, SLOPE = filter_taps()


def iota(shape, dim):
    return lax.broadcasted_iota(jnp.int32, shape, dim)


def band(distance, taps):
    table = jnp.zeros(distance.shape, jnp.float32)
    for tap in range(2 * RADIUS + 1):
        table = jnp.where(distance == tap - RADIUS, taps[tap], table)
    return table


def write_bands(band_x, band_y):
    d = iota((NXY, NXY), 0) - iota((NXY, NXY), 1)
    band_x[...] = jnp.concatenate([band(d, SMOOTH), band(d, SLOPE)], axis=1).astype(jnp.bfloat16)
    band_y[...] = jnp.concatenate([band(-d, SMOOTH), band(-d, SLOPE)], axis=0).astype(jnp.bfloat16)


def filter_planes(band_x, band_y, tomo, grads, start, count):
    planes = tomo[pl.ds(start, count)].reshape(count * NXY, NXY)
    along_x = jnp.dot(planes, band_x[...], preferred_element_type=jnp.float32).astype(jnp.bfloat16)
    for k in range(count):
        out = jnp.dot(
            band_y[...], along_x[k * NXY : (k + 1) * NXY], preferred_element_type=jnp.float32
        )
        grads[0, start + k] = out[:NXY, :NXY]
        grads[1, start + k] = out[NXY:, :NXY]
        grads[2, start + k] = out[:NXY, NXY:]


def filter_depth(grads):
    strips = NXY // 16

    def step(i, _):
        z0 = i // strips * GROUP
        rows = pl.ds(pl.multiple_of(i % strips * 16, 16), 16)
        for c in range(3):
            g = [grads[c, z0 + k, rows, :] for k in range(GROUP + 2 * RADIUS)]
            for k in range(GROUP):
                if c == 0:
                    grad = g[k + 4] - g[k + 2]
                    for t in (2, 3):
                        grad = grad + (SLOPE[3 + t] / SLOPE[4]) * (g[k + 3 + t] - g[k + 3 - t])
                else:
                    grad = g[k + 3]
                    for t in (1, 2, 3):
                        grad = grad + (SMOOTH[3 + t] / SMOOTH[3]) * (g[k + 3 + t] + g[k + 3 - t])
                grads[c, z0 + k, rows, :] = grad
        return 0

    lax.fori_loop(0, E // GROUP * strips, step, 0)


def write_shifts(offs, shifts):
    def element_row(ey, _):
        src = iota((NXY, NXY), 0)
        dst = iota((NXY, NXY), 1)
        for ex in range(PER_ROW):
            ox = offs[2, 0, ey * PER_ROW + ex]
            mine = dst // E == ex
            here = jnp.where(mine & (src == dst + ox), 1.0, 0.0)
            after = jnp.where(mine & (src == dst + ox + 1), 1.0, 0.0)
            shifts[ey, ex * NXY : (ex + 1) * NXY, :] = jnp.concatenate(
                [here, after - here], axis=1
            ).astype(jnp.bfloat16)
        return 0

    lax.fori_loop(0, PER_ROW, element_row, 0)


def warp_layer(offs, shifts, fields, volf, tomo_ref, grads, lhs, win, ysum, res_ref, row_done):
    ysum[...] = jnp.zeros_like(ysum)

    def gather_planes(ey, q):
        for ex in range(PER_ROW):
            oz = offs[0, 0, ey * PER_ROW + ex] + HALO
            oy = offs[1, 0, ey * PER_ROW + ex] + ey * E + YPAD
            two = []
            for k in range(2):
                z = jnp.minimum(2 * q + k + oz, VPLANES - 1)
                two.append(volf[z, pl.ds(oy, WIN), :])
            lhs[ey % 2, pl.ds(pl.multiple_of(q * 2 * WIN, 2 * WIN), 2 * WIN), ex * NXY : (ex + 1) * NXY] = (
                jnp.concatenate(two, axis=0).astype(jnp.bfloat16)
            )

    def gather_first(q, _):
        gather_planes(0, q)
        return 0

    lax.fori_loop(0, WPLANES // 2, gather_first, 0)

    def element_row(ey, _):
        after = jnp.minimum(ey + 1, PER_ROW - 1)
        gather_planes(after, WPLANES // 2 - 1)
        rows = WPLANES * WIN
        for r0 in range(0, rows, 480):
            r1 = min(r0 + 480, rows)
            out = jnp.dot(lhs[ey % 2, r0:r1, :], shifts[ey], preferred_element_type=jnp.float32)
            win[0, r0:r1, :] = out[:, :NXY]
            win[1, r0:r1, :] = out[:, NXY:]

        for half in range(2):
            pb = ((iota((16, NXY), 0).astype(jnp.float32)) + (16 * half + 0.5)) / E
            start, slope = [], []
            for c in range(3):
                planes = []
                for p in range(2):
                    at = p * 8 + c
                    lo = fields[ey, at : at + 1, :]
                    hi = fields[ey + 1, at : at + 1, :]
                    planes.append(lo * (1.0 - pb) + hi * pb)
                rise = (planes[1] - planes[0]) * (1.0 / E)
                start.append(planes[0] + 0.5 * rise)
                slope.append(rise)
            yrow = pl.multiple_of(ey * E + half * 16, 16)

            def planes_step(group, carry):
                sums, prefix = list(carry[:3]), list(carry[3:])
                z0 = group * GROUP
                gather_planes(after, group + half * (E // GROUP))

                def corner_rows(z):
                    r = pl.multiple_of(z * WIN, 8) + 16 * half
                    return (
                        win[0, pl.ds(r, 16), :],
                        win[1, pl.ds(r, 16), :],
                        win[0, pl.ds(r + 1, 16), :],
                        win[1, pl.ds(r + 1, 16), :],
                    )

                misfits = []
                lower = corner_rows(z0)
                for k in range(GROUP):
                    z = z0 + k
                    upper = corner_rows(z + 1)
                    zf = z.astype(jnp.float32)
                    wz, wy, wx = [start[c] + zf * slope[c] for c in range(3)]

                    def in_plane(rows):
                        a = rows[0] + wx * rows[1]
                        b = rows[2] + wx * rows[3]
                        return a + wy * (b - a)

                    t0 = in_plane(lower)
                    t1 = in_plane(upper)
                    ref = tomo_ref[z + RADIUS, pl.ds(yrow, 16), :].astype(jnp.float32)
                    misfit = t0 + wz * (t1 - t0) - ref
                    res_ref[z, pl.ds(yrow, 16), :] = misfit.astype(jnp.bfloat16)
                    misfits.append(misfit)
                    lower = upper
                for c in range(3):
                    for k in range(GROUP):
                        sums[c] = sums[c] + grads[c, z0 + k, pl.ds(yrow, 16), :] * misfits[k]
                        prefix[c] = prefix[c] + sums[c]
                return (*sums, *prefix)

            zero = jnp.zeros((16, NXY), jnp.float32)
            done = lax.fori_loop(0, E // GROUP, planes_step, (zero,) * 6)
            for c in range(3):
                scale = (SLOPE[4] if c == 0 else SMOOTH[3]) / E
                total = done[c] * scale
                top = ((E + 0.5) * total - done[3 + c] * scale) * (1.0 / E)
                for p, part in ((0, total - top), (1, top)):
                    for j, weight in ((0, 1.0 - pb), (1, pb)):
                        row = jnp.sum(part * weight, axis=0, keepdims=True)
                        at = p * 8 + c
                        ysum[ey + j, at : at + 1, :] = ysum[ey + j, at : at + 1, :] + row
        row_done(ey)
        return 0

    lax.fori_loop(0, PER_ROW, element_row, 0)


def node_lanes(iy):
    node = iota((NXY, NXY), 1) - NODES * iy
    voxel = iota((NXY, NXY), 0)
    upper = ((voxel % E).astype(jnp.float32) + 0.5) / E
    weight = jnp.where(voxel // E == node, 1.0 - upper, 0.0) + jnp.where(voxel // E + 1 == node, upper, 0.0)
    return jnp.where(node < NODES, weight, 0.0)


def node_fields(nodes, fields):
    for iy in range(NODES):
        fields[iy] = lax.dot_general(
            nodes[...],
            node_lanes(iy),
            (((1,), (1,)), ((), ())),
            preferred_element_type=jnp.float32,
            precision=lax.Precision.HIGHEST,
        )


def node_sums(ysum):
    total = jnp.zeros((16, NXY), jnp.float32)
    for iy in range(NODES):
        total = total + jnp.dot(
            ysum[iy], node_lanes(iy), preferred_element_type=jnp.float32, precision=lax.Precision.HIGHEST
        )
    return total


UP, DOWN, SIBLING, OTHER, RELAY, LOW_A, LOW_B, LOW_RELAY, HIGH_A, HIGH_B, HIGH_RELAY, NODE, TAIL = range(13)


def step_kernel(
    offs_hbm, sub_hbm, tomo_hbm, vol_hbm, res_hbm, rhs_ref,
    own, halo, tomo, res, volf, band_x, band_y, shifts, grads, lhs, win, ysum, fields, nodes, mine, above, sums, tail,
    offs, send, recv, local,
):
    bricks = lax.axis_size("brick")
    b = lax.axis_index("brick")
    s = lax.axis_index("scan")
    block = tomo_hbm.shape[0]
    has_above = b < bricks - 1
    has_below = b > 0
    odd = lax.rem(s, 2) == 1
    sibling = s + 1 - 2 * lax.rem(s, 2)
    other = lax.rem(s + 2, 4)

    def remote(kind, src, dst, brick, scan):
        return pltpu.make_async_remote_copy(
            src_ref=src,
            dst_ref=dst,
            send_sem=send.at[kind],
            recv_sem=recv.at[kind],
            device_id={"brick": brick, "scan": scan},
            device_id_type=pl.DeviceIdType.MESH,
        )

    def block_at(i):
        return tomo.at[pl.ds(RADIUS + block * i, block)]

    low_edge = tomo.at[pl.ds(0, RADIUS)]
    high_edge = tomo.at[pl.ds(RADIUS + E, RADIUS)]
    up = remote(UP, vol_hbm.at[0, pl.ds(E - HALO + 1, HALO - 1)], halo.at[0, pl.ds(1, HALO - 1)], b + 1, s)
    down = remote(DOWN, vol_hbm.at[0, pl.ds(0, HALO)], halo.at[1], b - 1, s)
    to_sibling = remote(SIBLING, tomo_hbm, block_at(s), b, sibling)
    to_other = remote(OTHER, tomo_hbm, block_at(s), b, other)
    relay = remote(RELAY, block_at(other), block_at(other), b, sibling)
    from_relay = remote(RELAY, block_at(lax.rem(sibling + 2, 4)), block_at(lax.rem(sibling + 2, 4)), b, sibling)
    from_sibling = remote(SIBLING, tomo_hbm, block_at(sibling), b, sibling)
    from_other = remote(OTHER, tomo_hbm, block_at(other), b, other)
    last_planes = tomo_hbm.at[pl.ds(block - RADIUS, RADIUS)]
    first_planes = tomo_hbm.at[pl.ds(0, RADIUS)]
    low_a = remote(LOW_A, last_planes, low_edge, b + 1, 3)
    low_b = remote(LOW_B, tomo.at[pl.ds(E, RADIUS)], low_edge, b + 1, 1)
    low_relay = remote(LOW_RELAY, low_edge, low_edge, b, sibling)
    high_a = remote(HIGH_A, first_planes, high_edge, b - 1, 0)
    high_b = remote(HIGH_B, tomo.at[pl.ds(RADIUS, RADIUS)], high_edge, b - 1, 2)
    high_relay = remote(HIGH_RELAY, high_edge, high_edge, b, sibling)
    node = remote(NODE, sub_hbm, above, b - 1, s)

    get_own = pltpu.make_async_copy(vol_hbm.at[0], own, local.at[0])
    get_tomo = pltpu.make_async_copy(tomo_hbm, block_at(s), local.at[1])
    get_offs = pltpu.make_async_copy(offs_hbm, offs, local.at[3 + PER_ROW])
    get_offs.start()
    get_sub = pltpu.make_async_copy(sub_hbm, mine, local.at[2])
    get_own.start()
    get_tomo.start()
    get_sub.start()

    barrier = pltpu.get_barrier_semaphore()

    def greet(brick, scan):
        pl.semaphore_signal(
            barrier, inc=1, device_id={"brick": brick, "scan": scan}, device_id_type=pl.DeviceIdType.MESH
        )

    greet(b, sibling)
    greet(b, other)

    @pl.when(has_above)
    def _():
        greet(b + 1, s)

    @pl.when(has_below)
    def _():
        greet(b - 1, s)

    pl.semaphore_wait(barrier, 2 + has_above.astype(jnp.int32) + has_below.astype(jnp.int32))

    to_other.start()
    to_sibling.start()

    @pl.when(has_above & (s == 3))
    def _():
        low_a.start()

    @pl.when(has_below & (s == 0))
    def _():
        high_a.start()

    @pl.when(has_below)
    def _():
        node.start()

    zeros_lo = jnp.zeros((YPAD, NXY), jnp.float32)
    zeros_hi = jnp.zeros((VROWS - YPAD - NXY, NXY), jnp.float32)

    def borders(z, _):
        volf[z, :YPAD] = zeros_lo
        volf[z, YPAD + NXY :] = zeros_hi
        return 0

    lax.fori_loop(0, VPLANES, borders, 0)
    nodes[...] = jnp.zeros_like(nodes)
    halo[0, 0] = jnp.zeros((NXY, NXY), jnp.bfloat16)
    get_sub.wait()
    for c in range(3):
        nodes[c : c + 1, : NODES * NODES] = mine[0, c]

    @pl.when(jnp.logical_not(has_below))
    def _():
        halo[0] = jnp.zeros((HALO, NXY, NXY), jnp.bfloat16)
        tomo[:RADIUS] = jnp.zeros((RADIUS, NXY, NXY), jnp.bfloat16)

    @pl.when(jnp.logical_not(has_above))
    def _():
        halo[1] = jnp.zeros((HALO, NXY, NXY), jnp.bfloat16)
        tomo[RADIUS + E :] = jnp.zeros((RADIUS, NXY, NXY), jnp.bfloat16)

    get_own.wait()

    def spread_own(z, _):
        volf[HALO + z, YPAD : YPAD + NXY] = own[z].astype(jnp.float32)
        return 0

    lax.fori_loop(0, E, spread_own, 0)

    def filter_block(i):
        filter_planes(band_x, band_y, tomo, grads, RADIUS + block * i, block)

    write_bands(band_x, band_y)
    get_tomo.wait()
    filter_block(s)

    from_other.wait_recv()
    relay.start()

    @pl.when(has_below)
    def _():
        down.start()

    @pl.when(has_above)
    def _():
        up.start()


    @pl.when(has_above & (s == 1))
    def _():
        low_b.start()

    @pl.when(has_below & (s == 2))
    def _():
        high_b.start()

    filter_block(other)
    from_sibling.wait_recv()
    filter_block(sibling)

    @pl.when(has_below & odd)
    def _():
        @pl.when(s == 3)
        def _():
            low_a.wait_recv()

        @pl.when(s == 1)
        def _():
            low_b.wait_recv()

        low_relay.start()

    @pl.when(has_above & jnp.logical_not(odd))
    def _():
        @pl.when(s == 0)
        def _():
            high_a.wait_recv()

        @pl.when(s == 2)
        def _():
            high_b.wait_recv()

        high_relay.start()

    get_offs.wait()
    write_shifts(offs, shifts)

    @pl.when(has_above)
    def _():
        node.wait_recv()
        for c in range(3):
            nodes[8 + c : 9 + c, : NODES * NODES] = above[0, c]

    node_fields(nodes, fields)
    from_relay.wait_recv()
    filter_block(lax.rem(sibling + 2, 4))

    @pl.when(has_below & jnp.logical_not(odd))
    def _():
        low_relay.wait_recv()

    @pl.when(has_above & odd)
    def _():
        high_relay.wait_recv()

    filter_planes(band_x, band_y, tomo, grads, 0, RADIUS)
    filter_planes(band_x, band_y, tomo, grads, RADIUS + E, RADIUS)
    filter_depth(grads)

    @pl.when(has_above)
    def _():
        down.wait_recv()

    @pl.when(has_below)
    def _():
        up.wait_recv()

    def spread_halo(z, _):
        volf[z, YPAD : YPAD + NXY] = halo[0, z].astype(jnp.float32)
        volf[HALO + E + z, YPAD : YPAD + NXY] = halo[1, z].astype(jnp.float32)
        return 0

    lax.fori_loop(0, HALO, spread_halo, 0)

    def put_row(ey):
        rows = pl.ds(pl.multiple_of(ey * E, E), E)
        return pltpu.make_async_copy(res.at[:, rows], res_hbm.at[:, rows], local.at[3 + ey])

    warp_layer(
        offs, shifts, fields, volf, tomo, grads, lhs, win, ysum, res, lambda ey: put_row(ey).start()
    )
    sums[...] = node_sums(ysum)
    to_above = remote(TAIL, sums.at[pl.ds(8, 8)], tail, b + 1, s)

    @pl.when(has_above)
    def _():
        to_above.start()

    to_other.wait_send()
    to_sibling.wait_send()
    relay.wait_send()

    @pl.when(has_above & (s == 3))
    def _():
        low_a.wait_send()

    @pl.when(has_above & (s == 1))
    def _():
        low_b.wait_send()

    @pl.when(has_below & (s == 0))
    def _():
        high_a.wait_send()

    @pl.when(has_below & (s == 2))
    def _():
        high_b.wait_send()

    @pl.when(has_below & odd)
    def _():
        low_relay.wait_send()

    @pl.when(has_above & jnp.logical_not(odd))
    def _():
        high_relay.wait_send()

    @pl.when(has_above)
    def _():
        up.wait_send()

    @pl.when(has_below)
    def _():
        down.wait_send()
        node.wait_send()

    for ey in range(PER_ROW):
        put_row(ey).wait()

    @pl.when(jnp.logical_not(has_below))
    def _():
        tail[...] = jnp.zeros_like(tail)

    @pl.when(has_below)
    def _():
        to_above.wait_recv()

    final = sums[:8] + tail[...]
    for c in range(3):
        rhs_ref[0, c] = final[c : c + 1, : NODES * NODES]

    @pl.when(has_above)
    def _():
        to_above.wait_send()


def body(tomogram, deformed, subvoxel, offsets):
    tall = E + 2 * RADIUS
    smem = pl.BlockSpec(memory_space=pltpu.SMEM)
    vmem = pl.BlockSpec(memory_space=pltpu.VMEM)
    hbm = pl.BlockSpec(memory_space=pltpu.HBM)
    residual, node_rhs = pl.pallas_call(
        step_kernel,
        out_shape=(
            jax.ShapeDtypeStruct((E, NXY, NXY), jnp.bfloat16),
            jax.ShapeDtypeStruct(subvoxel.shape, jnp.float32),
        ),
        in_specs=[hbm, hbm, hbm, hbm],
        out_specs=(hbm, vmem),
        scratch_shapes=[
            pltpu.VMEM((E, NXY, NXY), jnp.bfloat16),
            pltpu.VMEM((2, HALO, NXY, NXY), jnp.bfloat16),
            pltpu.VMEM((tall, NXY, NXY), jnp.bfloat16),
            pltpu.VMEM((E, NXY, NXY), jnp.bfloat16),
            pltpu.VMEM((VPLANES, VROWS, NXY), jnp.float32),
            pltpu.VMEM((NXY, 2 * NXY), jnp.bfloat16),
            pltpu.VMEM((2 * NXY, NXY), jnp.bfloat16),
            pltpu.VMEM((PER_ROW, PER_ROW * NXY, 2 * NXY), jnp.bfloat16),
            pltpu.VMEM((3, tall, NXY, NXY), jnp.float32),
            pltpu.VMEM((2, WPLANES * WIN, PER_ROW * NXY), jnp.bfloat16),
            pltpu.VMEM((2, WPLANES * WIN, NXY), jnp.float32),
            pltpu.VMEM((NODES, 16, NXY), jnp.float32),
            pltpu.VMEM((NODES, 16, NXY), jnp.float32),
            pltpu.VMEM((16, NXY), jnp.float32),
            pltpu.VMEM(subvoxel.shape, jnp.float32),
            pltpu.VMEM(subvoxel.shape, jnp.float32),
            pltpu.VMEM((16, NXY), jnp.float32),
            pltpu.VMEM((8, NXY), jnp.float32),
            pltpu.SMEM((3, 1, PER_ROW * PER_ROW), jnp.int32),
            pltpu.SemaphoreType.DMA((13,)),
            pltpu.SemaphoreType.DMA((13,)),
            pltpu.SemaphoreType.DMA((4 + PER_ROW,)),
        ],
        compiler_params=pltpu.CompilerParams(
            collective_id=0, has_side_effects=True, vmem_limit_bytes=50 << 20
        ),
    )(
        *[
            pltpu.with_memory_space_constraint(x, pltpu.HBM)
            for x in (offsets.transpose(1, 0, 2), subvoxel, tomogram, deformed)
        ],
    )
    return residual[None], node_rhs


def solution(mesh):
    return jax.shard_map(
        body,
        mesh=mesh,
        in_specs=(
            P(("brick", "scan"), None, None),
            P("scan", "brick", None, None),
            P("scan", None, "brick", None),
            P("scan", None, "brick"),
        ),
        out_specs=(P("scan", "brick", None, None), P("scan", None, "brick", None)),
        check_vma=False,
    )
```

```python
import jax
import jax.numpy as jnp
import ml_dtypes
import numpy as np
from jax import lax
from jax.experimental import pallas as pl
from jax.experimental.pallas import tpu as pltpu
from jax.sharding import PartitionSpec as P

E = 32
HALO = 16
RADIUS = 3
NXY = 128
PER_ROW = 4
NODES = 5
GAUSS_SIGMA = 1.0

WIN = 40
WPLANES = 34
VPLANES = E + 2 * HALO
YPAD = HALO
VROWS = 168
GROUP = 4


def filter_taps():
    tap_pos = np.arange(-RADIUS, RADIUS + 1).astype(np.float32)
    gaussian = np.exp(-tap_pos * tap_pos / np.float32(2.0 * GAUSS_SIGMA * GAUSS_SIGMA))
    smooth = gaussian / np.sum(gaussian)
    slope = tap_pos * gaussian / np.sum(tap_pos * tap_pos * gaussian)
    return (
        [float(v) for v in smooth.astype(ml_dtypes.bfloat16)],
        [float(v) for v in slope.astype(ml_dtypes.bfloat16)],
    )


SMOOTH, SLOPE = filter_taps()


def iota(shape, dim):
    return lax.broadcasted_iota(jnp.int32, shape, dim)


def band(distance, taps):
    table = jnp.zeros(distance.shape, jnp.float32)
    for tap in range(2 * RADIUS + 1):
        table = jnp.where(distance == tap - RADIUS, taps[tap], table)
    return table


def write_bands(band_x, band_y):
    d = iota((NXY, NXY), 0) - iota((NXY, NXY), 1)
    band_x[...] = jnp.concatenate([band(d, SMOOTH), band(d, SLOPE)], axis=1).astype(jnp.bfloat16)
    band_y[...] = jnp.concatenate([band(-d, SMOOTH), band(-d, SLOPE)], axis=0).astype(jnp.bfloat16)


def filter_planes(band_x, band_y, tomo, grads, start, count):
    planes = tomo[pl.ds(start, count)].reshape(count * NXY, NXY)
    along_x = jnp.dot(planes, band_x[...], preferred_element_type=jnp.float32).astype(jnp.bfloat16)
    for k in range(count):
        out = jnp.dot(
            band_y[...], along_x[k * NXY : (k + 1) * NXY], preferred_element_type=jnp.float32
        )
        grads[0, start + k] = out[:NXY, :NXY]
        grads[1, start + k] = out[NXY:, :NXY]
        grads[2, start + k] = out[:NXY, NXY:]


def filter_depth(grads):
    strips = NXY // 16

    def step(i, _):
        z0 = i // strips * GROUP
        rows = pl.ds(pl.multiple_of(i % strips * 16, 16), 16)
        for c in range(3):
            g = [grads[c, z0 + k, rows, :] for k in range(GROUP + 2 * RADIUS)]
            for k in range(GROUP):
                if c == 0:
                    grad = g[k + 4] - g[k + 2]
                    for t in (2, 3):
                        grad = grad + (SLOPE[3 + t] / SLOPE[4]) * (g[k + 3 + t] - g[k + 3 - t])
                else:
                    grad = g[k + 3]
                    for t in (1, 2, 3):
                        grad = grad + (SMOOTH[3 + t] / SMOOTH[3]) * (g[k + 3 + t] + g[k + 3 - t])
                grads[c, z0 + k, rows, :] = grad
        return 0

    lax.fori_loop(0, E // GROUP * strips, step, 0)


def write_shifts(offs, shifts):
    def element_row(ey, _):
        src = iota((NXY, NXY), 0)
        dst = iota((NXY, NXY), 1)
        for ex in range(PER_ROW):
            ox = offs[2, 0, ey * PER_ROW + ex]
            mine = dst // E == ex
            here = jnp.where(mine & (src == dst + ox), 1.0, 0.0)
            after = jnp.where(mine & (src == dst + ox + 1), 1.0, 0.0)
            shifts[ey, ex * NXY : (ex + 1) * NXY, :] = jnp.concatenate(
                [here, after - here], axis=1
            ).astype(jnp.bfloat16)
        return 0

    lax.fori_loop(0, PER_ROW, element_row, 0)


def warp_layer(offs, shifts, fields, volf, tomo_ref, grads, lhs, win, ysum, res_ref):
    ysum[...] = jnp.zeros_like(ysum)

    def gather_planes(ey, q):
        for ex in range(PER_ROW):
            oz = offs[0, 0, ey * PER_ROW + ex] + HALO
            oy = offs[1, 0, ey * PER_ROW + ex] + ey * E + YPAD
            two = []
            for k in range(2):
                z = jnp.minimum(2 * q + k + oz, VPLANES - 1)
                two.append(volf[z, pl.ds(oy, WIN), :])
            lhs[ey % 2, pl.ds(pl.multiple_of(q * 2 * WIN, 2 * WIN), 2 * WIN), ex * NXY : (ex + 1) * NXY] = (
                jnp.concatenate(two, axis=0).astype(jnp.bfloat16)
            )

    def gather_first(q, _):
        gather_planes(0, q)
        return 0

    lax.fori_loop(0, WPLANES // 2, gather_first, 0)

    def element_row(ey, _):
        after = jnp.minimum(ey + 1, PER_ROW - 1)
        gather_planes(after, WPLANES // 2 - 1)
        rows = WPLANES * WIN
        for r0 in range(0, rows, 480):
            r1 = min(r0 + 480, rows)
            out = jnp.dot(lhs[ey % 2, r0:r1, :], shifts[ey], preferred_element_type=jnp.float32)
            win[0, r0:r1, :] = out[:, :NXY]
            win[1, r0:r1, :] = out[:, NXY:]

        for half in range(2):
            pb = ((iota((16, NXY), 0).astype(jnp.float32)) + (16 * half + 0.5)) / E
            start, slope = [], []
            for c in range(3):
                planes = []
                for p in range(2):
                    at = p * 8 + c
                    lo = fields[ey, at : at + 1, :]
                    hi = fields[ey + 1, at : at + 1, :]
                    planes.append(lo * (1.0 - pb) + hi * pb)
                rise = (planes[1] - planes[0]) * (1.0 / E)
                start.append(planes[0] + 0.5 * rise)
                slope.append(rise)
            yrow = pl.multiple_of(ey * E + half * 16, 16)

            def planes_step(group, carry):
                sums, prefix = list(carry[:3]), list(carry[3:])
                z0 = group * GROUP
                gather_planes(after, group + half * (E // GROUP))

                def corner_rows(z):
                    r = pl.multiple_of(z * WIN, 8) + 16 * half
                    return (
                        win[0, pl.ds(r, 16), :],
                        win[1, pl.ds(r, 16), :],
                        win[0, pl.ds(r + 1, 16), :],
                        win[1, pl.ds(r + 1, 16), :],
                    )

                lower = corner_rows(z0)
                for k in range(GROUP):
                    z = z0 + k
                    upper = corner_rows(z + 1)
                    zf = z.astype(jnp.float32)
                    wz, wy, wx = [start[c] + zf * slope[c] for c in range(3)]

                    def in_plane(rows):
                        a = rows[0] + wx * rows[1]
                        b = rows[2] + wx * rows[3]
                        return a + wy * (b - a)

                    t0 = in_plane(lower)
                    t1 = in_plane(upper)
                    ref = tomo_ref[z + RADIUS, pl.ds(yrow, 16), :].astype(jnp.float32)
                    misfit = t0 + wz * (t1 - t0) - ref
                    res_ref[z, pl.ds(yrow, 16), :] = misfit.astype(jnp.bfloat16)
                    for c in range(3):
                        sums[c] = sums[c] + grads[c, z, pl.ds(yrow, 16), :] * misfit
                        prefix[c] = prefix[c] + sums[c]
                    lower = upper
                return (*sums, *prefix)

            zero = jnp.zeros((16, NXY), jnp.float32)
            done = lax.fori_loop(0, E // GROUP, planes_step, (zero,) * 6)
            for c in range(3):
                scale = (SLOPE[4] if c == 0 else SMOOTH[3]) / E
                total = done[c] * scale
                top = ((E + 0.5) * total - done[3 + c] * scale) * (1.0 / E)
                for p, part in ((0, total - top), (1, top)):
                    for j, weight in ((0, 1.0 - pb), (1, pb)):
                        row = jnp.sum(part * weight, axis=0, keepdims=True)
                        at = p * 8 + c
                        ysum[ey + j, at : at + 1, :] = ysum[ey + j, at : at + 1, :] + row
        return 0

    lax.fori_loop(0, PER_ROW, element_row, 0)


def node_lanes(iy):
    node = iota((NXY, NXY), 1) - NODES * iy
    voxel = iota((NXY, NXY), 0)
    upper = ((voxel % E).astype(jnp.float32) + 0.5) / E
    weight = jnp.where(voxel // E == node, 1.0 - upper, 0.0) + jnp.where(voxel // E + 1 == node, upper, 0.0)
    return jnp.where(node < NODES, weight, 0.0)


def node_fields(nodes, fields, lanes):
    for iy in range(NODES):
        lanes[iy] = node_lanes(iy)
        fields[iy] = lax.dot_general(
            nodes[...],
            lanes[iy],
            (((1,), (1,)), ((), ())),
            preferred_element_type=jnp.float32,
            precision=lax.Precision.HIGHEST,
        )


def node_sums(ysum, lanes):
    total = jnp.zeros((16, NXY), jnp.float32)
    for iy in range(NODES):
        total = total + jnp.dot(
            ysum[iy], lanes[iy], preferred_element_type=jnp.float32, precision=lax.Precision.HIGHEST
        )
    return total


UP, DOWN, SIBLING, OTHER, RELAY, LOW_A, LOW_B, LOW_RELAY, HIGH_A, HIGH_B, HIGH_RELAY, NODE, TAIL = range(13)


def step_kernel(
    offs_hbm, sub_hbm, tomo_hbm, vol_hbm, res, rhs_ref,
    own, halo, tomo, lanes, volf, band_x, band_y, shifts, grads, lhs, win, ysum, fields, nodes, mine, above, sums, tail,
    offs, send, recv, local,
):
    bricks = lax.axis_size("brick")
    b = lax.axis_index("brick")
    s = lax.axis_index("scan")
    block = tomo_hbm.shape[0]
    has_above = b < bricks - 1
    has_below = b > 0
    odd = lax.rem(s, 2) == 1
    sibling = s + 1 - 2 * lax.rem(s, 2)
    other = lax.rem(s + 2, 4)

    def remote(kind, src, dst, brick, scan):
        return pltpu.make_async_remote_copy(
            src_ref=src,
            dst_ref=dst,
            send_sem=send.at[kind],
            recv_sem=recv.at[kind],
            device_id={"brick": brick, "scan": scan},
            device_id_type=pl.DeviceIdType.MESH,
        )

    def block_at(i):
        return tomo.at[pl.ds(RADIUS + block * i, block)]

    low_edge = tomo.at[pl.ds(0, RADIUS)]
    high_edge = tomo.at[pl.ds(RADIUS + E, RADIUS)]
    up = remote(UP, vol_hbm.at[0, pl.ds(E - HALO + 1, HALO - 1)], halo.at[0, pl.ds(1, HALO - 1)], b + 1, s)
    down = remote(DOWN, vol_hbm.at[0, pl.ds(0, HALO)], halo.at[1], b - 1, s)
    to_sibling = remote(SIBLING, tomo_hbm, block_at(s), b, sibling)
    to_other = remote(OTHER, tomo_hbm, block_at(s), b, other)
    relay = remote(RELAY, block_at(other), block_at(other), b, sibling)
    from_relay = remote(RELAY, block_at(lax.rem(sibling + 2, 4)), block_at(lax.rem(sibling + 2, 4)), b, sibling)
    from_sibling = remote(SIBLING, tomo_hbm, block_at(sibling), b, sibling)
    from_other = remote(OTHER, tomo_hbm, block_at(other), b, other)
    last_planes = tomo_hbm.at[pl.ds(block - RADIUS, RADIUS)]
    first_planes = tomo_hbm.at[pl.ds(0, RADIUS)]
    low_a = remote(LOW_A, last_planes, low_edge, b + 1, 3)
    low_b = remote(LOW_B, tomo.at[pl.ds(E, RADIUS)], low_edge, b + 1, 1)
    low_relay = remote(LOW_RELAY, low_edge, low_edge, b, sibling)
    high_a = remote(HIGH_A, first_planes, high_edge, b - 1, 0)
    high_b = remote(HIGH_B, tomo.at[pl.ds(RADIUS, RADIUS)], high_edge, b - 1, 2)
    high_relay = remote(HIGH_RELAY, high_edge, high_edge, b, sibling)
    node = remote(NODE, sub_hbm, above, b - 1, s)

    get_own = pltpu.make_async_copy(vol_hbm.at[0], own, local.at[0])
    get_tomo = pltpu.make_async_copy(tomo_hbm, block_at(s), local.at[1])
    get_offs = pltpu.make_async_copy(offs_hbm, offs, local.at[3])
    get_offs.start()
    get_sub = pltpu.make_async_copy(sub_hbm, mine, local.at[2])
    get_own.start()
    get_tomo.start()
    get_sub.start()

    barrier = pltpu.get_barrier_semaphore()

    def greet(brick, scan):
        pl.semaphore_signal(
            barrier, inc=1, device_id={"brick": brick, "scan": scan}, device_id_type=pl.DeviceIdType.MESH
        )

    greet(b, sibling)
    greet(b, other)

    @pl.when(has_above)
    def _():
        greet(b + 1, s)

    @pl.when(has_below)
    def _():
        greet(b - 1, s)

    pl.semaphore_wait(barrier, 2 + has_above.astype(jnp.int32) + has_below.astype(jnp.int32))

    @pl.when(has_above & (s == 3))
    def _():
        low_a.start()

    @pl.when(has_below & (s == 0))
    def _():
        high_a.start()

    to_other.start()
    to_sibling.start()

    @pl.when(has_below)
    def _():
        node.start()

    zeros_lo = jnp.zeros((YPAD, NXY), jnp.float32)
    zeros_hi = jnp.zeros((VROWS - YPAD - NXY, NXY), jnp.float32)

    def borders(z, _):
        volf[z, :YPAD] = zeros_lo
        volf[z, YPAD + NXY :] = zeros_hi
        return 0

    lax.fori_loop(0, VPLANES, borders, 0)
    nodes[...] = jnp.zeros_like(nodes)
    halo[0, 0] = jnp.zeros((NXY, NXY), jnp.bfloat16)
    get_sub.wait()
    for c in range(3):
        nodes[c : c + 1, : NODES * NODES] = mine[0, c]

    @pl.when(jnp.logical_not(has_below))
    def _():
        halo[0] = jnp.zeros((HALO, NXY, NXY), jnp.bfloat16)
        tomo[:RADIUS] = jnp.zeros((RADIUS, NXY, NXY), jnp.bfloat16)

    @pl.when(jnp.logical_not(has_above))
    def _():
        halo[1] = jnp.zeros((HALO, NXY, NXY), jnp.bfloat16)
        tomo[RADIUS + E :] = jnp.zeros((RADIUS, NXY, NXY), jnp.bfloat16)

    get_own.wait()

    def spread_own(z, _):
        volf[HALO + z, YPAD : YPAD + NXY] = own[z].astype(jnp.float32)
        return 0

    lax.fori_loop(0, E, spread_own, 0)

    def filter_block(i):
        filter_planes(band_x, band_y, tomo, grads, RADIUS + block * i, block)

    write_bands(band_x, band_y)
    get_tomo.wait()
    filter_block(s)

    from_other.wait_recv()

    @pl.when(has_below)
    def _():
        down.start()

    @pl.when(has_above)
    def _():
        up.start()

    relay.start()


    @pl.when(has_above & (s == 1))
    def _():
        low_b.start()

    @pl.when(has_below & (s == 2))
    def _():
        high_b.start()

    filter_block(other)
    from_sibling.wait_recv()
    filter_block(sibling)

    @pl.when(has_below & odd)
    def _():
        @pl.when(s == 3)
        def _():
            low_a.wait_recv()

        @pl.when(s == 1)
        def _():
            low_b.wait_recv()

        low_relay.start()

    @pl.when(has_above & jnp.logical_not(odd))
    def _():
        @pl.when(s == 0)
        def _():
            high_a.wait_recv()

        @pl.when(s == 2)
        def _():
            high_b.wait_recv()

        high_relay.start()

    get_offs.wait()
    write_shifts(offs, shifts)

    @pl.when(has_above)
    def _():
        node.wait_recv()
        for c in range(3):
            nodes[8 + c : 9 + c, : NODES * NODES] = above[0, c]

    node_fields(nodes, fields, lanes)
    from_relay.wait_recv()
    filter_block(lax.rem(sibling + 2, 4))

    @pl.when(has_below & jnp.logical_not(odd))
    def _():
        low_relay.wait_recv()

    @pl.when(has_above & odd)
    def _():
        high_relay.wait_recv()

    filter_planes(band_x, band_y, tomo, grads, 0, RADIUS)
    filter_planes(band_x, band_y, tomo, grads, RADIUS + E, RADIUS)
    filter_depth(grads)

    @pl.when(has_above)
    def _():
        down.wait_recv()

    @pl.when(has_below)
    def _():
        up.wait_recv()

    def spread_halo(z, _):
        volf[z, YPAD : YPAD + NXY] = halo[0, z].astype(jnp.float32)
        volf[HALO + E + z, YPAD : YPAD + NXY] = halo[1, z].astype(jnp.float32)
        return 0

    lax.fori_loop(0, HALO, spread_halo, 0)

    warp_layer(
        offs, shifts, fields, volf, tomo, grads, lhs, win, ysum, res
    )
    sums[...] = node_sums(ysum, lanes)
    to_above = remote(TAIL, sums.at[pl.ds(8, 8)], tail, b + 1, s)

    @pl.when(has_above)
    def _():
        to_above.start()

    to_other.wait_send()
    to_sibling.wait_send()
    relay.wait_send()

    @pl.when(has_above & (s == 3))
    def _():
        low_a.wait_send()

    @pl.when(has_above & (s == 1))
    def _():
        low_b.wait_send()

    @pl.when(has_below & (s == 0))
    def _():
        high_a.wait_send()

    @pl.when(has_below & (s == 2))
    def _():
        high_b.wait_send()

    @pl.when(has_below & odd)
    def _():
        low_relay.wait_send()

    @pl.when(has_above & jnp.logical_not(odd))
    def _():
        high_relay.wait_send()

    @pl.when(has_above)
    def _():
        up.wait_send()

    @pl.when(has_below)
    def _():
        down.wait_send()
        node.wait_send()

    @pl.when(jnp.logical_not(has_below))
    def _():
        tail[...] = jnp.zeros_like(tail)

    @pl.when(has_below)
    def _():
        to_above.wait_recv()

    final = sums[:8] + tail[...]
    for c in range(3):
        rhs_ref[0, c] = final[c : c + 1, : NODES * NODES]

    @pl.when(has_above)
    def _():
        to_above.wait_send()


def body(tomogram, deformed, subvoxel, offsets):
    tall = E + 2 * RADIUS
    smem = pl.BlockSpec(memory_space=pltpu.SMEM)
    vmem = pl.BlockSpec(memory_space=pltpu.VMEM)
    hbm = pl.BlockSpec(memory_space=pltpu.HBM)
    residual, node_rhs = pl.pallas_call(
        step_kernel,
        out_shape=(
            jax.ShapeDtypeStruct((E, NXY, NXY), jnp.bfloat16),
            jax.ShapeDtypeStruct(subvoxel.shape, jnp.float32),
        ),
        in_specs=[hbm, hbm, hbm, hbm],
        out_specs=(vmem, vmem),
        scratch_shapes=[
            pltpu.VMEM((E, NXY, NXY), jnp.bfloat16),
            pltpu.VMEM((2, HALO, NXY, NXY), jnp.bfloat16),
            pltpu.VMEM((tall, NXY, NXY), jnp.bfloat16),
            pltpu.VMEM((NODES, NXY, NXY), jnp.float32),
            pltpu.VMEM((VPLANES, VROWS, NXY), jnp.float32),
            pltpu.VMEM((NXY, 2 * NXY), jnp.bfloat16),
            pltpu.VMEM((2 * NXY, NXY), jnp.bfloat16),
            pltpu.VMEM((PER_ROW, PER_ROW * NXY, 2 * NXY), jnp.bfloat16),
            pltpu.VMEM((3, tall, NXY, NXY), jnp.float32),
            pltpu.VMEM((2, WPLANES * WIN, PER_ROW * NXY), jnp.bfloat16),
            pltpu.VMEM((2, WPLANES * WIN, NXY), jnp.float32),
            pltpu.VMEM((NODES, 16, NXY), jnp.float32),
            pltpu.VMEM((NODES, 16, NXY), jnp.float32),
            pltpu.VMEM((16, NXY), jnp.float32),
            pltpu.VMEM(subvoxel.shape, jnp.float32),
            pltpu.VMEM(subvoxel.shape, jnp.float32),
            pltpu.VMEM((16, NXY), jnp.float32),
            pltpu.VMEM((8, NXY), jnp.float32),
            pltpu.SMEM((3, 1, PER_ROW * PER_ROW), jnp.int32),
            pltpu.SemaphoreType.DMA((13,)),
            pltpu.SemaphoreType.DMA((13,)),
            pltpu.SemaphoreType.DMA((4,)),
        ],
        compiler_params=pltpu.CompilerParams(
            collective_id=0, has_side_effects=True, vmem_limit_bytes=50 << 20
        ),
    )(
        *[
            pltpu.with_memory_space_constraint(x, pltpu.HBM)
            for x in (offsets.transpose(1, 0, 2), subvoxel, tomogram, deformed)
        ],
    )
    return residual[None], node_rhs


def solution(mesh):
    return jax.shard_map(
        body,
        mesh=mesh,
        in_specs=(
            P(("brick", "scan"), None, None),
            P("scan", "brick", None, None),
            P("scan", None, "brick", None),
            P("scan", None, "brick"),
        ),
        out_specs=(P("scan", "brick", None, None), P("scan", None, "brick", None)),
        check_vma=False,
    )
```

```python
import jax
import jax.numpy as jnp
import ml_dtypes
import numpy as np
from jax import lax
from jax.experimental import pallas as pl
from jax.experimental.pallas import tpu as pltpu
from jax.sharding import PartitionSpec as P

E = 32
HALO = 16
RADIUS = 3
NXY = 128
PER_ROW = 4
NODES = 5
GAUSS_SIGMA = 1.0

WIN = 40
WPLANES = 34
VPLANES = E + 2 * HALO
YPAD = HALO
VROWS = 168
GROUP = 4


def filter_taps():
    tap_pos = np.arange(-RADIUS, RADIUS + 1).astype(np.float32)
    gaussian = np.exp(-tap_pos * tap_pos / np.float32(2.0 * GAUSS_SIGMA * GAUSS_SIGMA))
    smooth = gaussian / np.sum(gaussian)
    slope = tap_pos * gaussian / np.sum(tap_pos * tap_pos * gaussian)
    return (
        [float(v) for v in smooth.astype(ml_dtypes.bfloat16)],
        [float(v) for v in slope.astype(ml_dtypes.bfloat16)],
    )


SMOOTH, SLOPE = filter_taps()


def iota(shape, dim):
    return lax.broadcasted_iota(jnp.int32, shape, dim)


def band(distance, taps):
    table = jnp.zeros(distance.shape, jnp.float32)
    for tap in range(2 * RADIUS + 1):
        table = jnp.where(distance == tap - RADIUS, taps[tap], table)
    return table


def write_bands(band_x, band_y):
    d = iota((NXY, NXY), 0) - iota((NXY, NXY), 1)
    band_x[...] = jnp.concatenate([band(d, SMOOTH), band(d, SLOPE)], axis=1).astype(jnp.bfloat16)
    band_y[...] = jnp.concatenate([band(-d, SMOOTH), band(-d, SLOPE)], axis=0).astype(jnp.bfloat16)


def filter_planes(band_x, band_y, tomo, grads, start, count):
    planes = tomo[pl.ds(start, count)].reshape(count * NXY, NXY)
    along_x = jnp.dot(planes, band_x[...], preferred_element_type=jnp.float32).astype(jnp.bfloat16)
    for k in range(count):
        out = jnp.dot(
            band_y[...], along_x[k * NXY : (k + 1) * NXY], preferred_element_type=jnp.float32
        )
        grads[0, start + k] = out[:NXY, :NXY]
        grads[1, start + k] = out[NXY:, :NXY]
        grads[2, start + k] = out[:NXY, NXY:]


def filter_depth(grads):
    strips = NXY // 16

    def step(i, _):
        z0 = i // strips * GROUP
        rows = pl.ds(pl.multiple_of(i % strips * 16, 16), 16)
        for c in range(3):
            g = [grads[c, z0 + k, rows, :] for k in range(GROUP + 2 * RADIUS)]
            for k in range(GROUP):
                if c == 0:
                    grad = g[k + 4] - g[k + 2]
                    for t in (2, 3):
                        grad = grad + (SLOPE[3 + t] / SLOPE[4]) * (g[k + 3 + t] - g[k + 3 - t])
                else:
                    grad = g[k + 3]
                    for t in (1, 2, 3):
                        grad = grad + (SMOOTH[3 + t] / SMOOTH[3]) * (g[k + 3 + t] + g[k + 3 - t])
                grads[c, z0 + k, rows, :] = grad
        return 0

    lax.fori_loop(0, E // GROUP * strips, step, 0)


def write_shifts(offs, shifts):
    def element_row(ey, _):
        src = iota((NXY, NXY), 0)
        dst = iota((NXY, NXY), 1)
        for ex in range(PER_ROW):
            ox = offs[2, 0, ey * PER_ROW + ex]
            mine = dst // E == ex
            here = jnp.where(mine & (src == dst + ox), 1.0, 0.0)
            after = jnp.where(mine & (src == dst + ox + 1), 1.0, 0.0)
            shifts[ey, ex * NXY : (ex + 1) * NXY, :] = jnp.concatenate(
                [here, after - here], axis=1
            ).astype(jnp.bfloat16)
        return 0

    lax.fori_loop(0, PER_ROW, element_row, 0)


def warp_layer(offs, shifts, fields, volf, tomo_ref, grads, lhs, win, ysum, res_ref):
    ysum[...] = jnp.zeros_like(ysum)

    def gather_planes(ey, q):
        for ex in range(PER_ROW):
            oz = offs[0, 0, ey * PER_ROW + ex] + HALO
            oy = offs[1, 0, ey * PER_ROW + ex] + ey * E + YPAD
            two = []
            for k in range(2):
                z = jnp.minimum(2 * q + k + oz, VPLANES - 1)
                two.append(volf[z, pl.ds(oy, WIN), :])
            lhs[ey % 2, pl.ds(pl.multiple_of(q * 2 * WIN, 2 * WIN), 2 * WIN), ex * NXY : (ex + 1) * NXY] = (
                jnp.concatenate(two, axis=0).astype(jnp.bfloat16)
            )

    def gather_first(q, _):
        gather_planes(0, q)
        return 0

    lax.fori_loop(0, WPLANES // 2, gather_first, 0)

    def element_row(ey, _):
        after = jnp.minimum(ey + 1, PER_ROW - 1)
        gather_planes(after, WPLANES // 2 - 1)
        rows = WPLANES * WIN
        for r0 in range(0, rows, 480):
            r1 = min(r0 + 480, rows)
            out = jnp.dot(lhs[ey % 2, r0:r1, :], shifts[ey], preferred_element_type=jnp.float32)
            win[0, r0:r1, :] = out[:, :NXY]
            win[1, r0:r1, :] = out[:, NXY:]

        for half in range(2):
            pb = ((iota((16, NXY), 0).astype(jnp.float32)) + (16 * half + 0.5)) / E
            start, slope = [], []
            for c in range(3):
                planes = []
                for p in range(2):
                    at = p * 8 + c
                    lo = fields[ey, at : at + 1, :]
                    hi = fields[ey + 1, at : at + 1, :]
                    planes.append(lo * (1.0 - pb) + hi * pb)
                rise = (planes[1] - planes[0]) * (1.0 / E)
                start.append(planes[0] + 0.5 * rise)
                slope.append(rise)
            yrow = pl.multiple_of(ey * E + half * 16, 16)

            def planes_step(group, carry):
                sums, prefix = list(carry[:3]), list(carry[3:])
                z0 = group * GROUP
                gather_planes(after, group + half * (E // GROUP))

                def corner_rows(z):
                    r = pl.multiple_of(z * WIN, 8) + 16 * half
                    return (
                        win[0, pl.ds(r, 16), :],
                        win[1, pl.ds(r, 16), :],
                        win[0, pl.ds(r + 1, 16), :],
                        win[1, pl.ds(r + 1, 16), :],
                    )

                lower = corner_rows(z0)
                for k in range(GROUP):
                    z = z0 + k
                    upper = corner_rows(z + 1)
                    zf = z.astype(jnp.float32)
                    wz, wy, wx = [start[c] + zf * slope[c] for c in range(3)]

                    def in_plane(rows):
                        a = rows[0] + wx * rows[1]
                        b = rows[2] + wx * rows[3]
                        return a + wy * (b - a)

                    t0 = in_plane(lower)
                    t1 = in_plane(upper)
                    ref = tomo_ref[z + RADIUS, pl.ds(yrow, 16), :].astype(jnp.float32)
                    misfit = t0 + wz * (t1 - t0) - ref
                    res_ref[z, pl.ds(yrow, 16), :] = misfit.astype(jnp.bfloat16)
                    for c in range(3):
                        sums[c] = sums[c] + grads[c, z, pl.ds(yrow, 16), :] * misfit
                        prefix[c] = prefix[c] + sums[c]
                    lower = upper
                return (*sums, *prefix)

            zero = jnp.zeros((16, NXY), jnp.float32)
            done = lax.fori_loop(0, E // GROUP, planes_step, (zero,) * 6)
            for c in range(3):
                scale = (SLOPE[4] if c == 0 else SMOOTH[3]) / E
                total = done[c] * scale
                top = ((E + 0.5) * total - done[3 + c] * scale) * (1.0 / E)
                for p, part in ((0, total - top), (1, top)):
                    for j, weight in ((0, 1.0 - pb), (1, pb)):
                        row = jnp.sum(part * weight, axis=0, keepdims=True)
                        at = p * 8 + c
                        ysum[ey + j, at : at + 1, :] = ysum[ey + j, at : at + 1, :] + row
        return 0

    lax.fori_loop(0, PER_ROW, element_row, 0)


def node_lanes(iy):
    node = iota((NXY, NXY), 1) - NODES * iy
    voxel = iota((NXY, NXY), 0)
    upper = ((voxel % E).astype(jnp.float32) + 0.5) / E
    weight = jnp.where(voxel // E == node, 1.0 - upper, 0.0) + jnp.where(voxel // E + 1 == node, upper, 0.0)
    return jnp.where(node < NODES, weight, 0.0)


def node_fields(nodes, fields, lanes):
    for iy in range(NODES):
        lanes[iy] = node_lanes(iy)
        fields[iy] = lax.dot_general(
            nodes[...],
            lanes[iy],
            (((1,), (1,)), ((), ())),
            preferred_element_type=jnp.float32,
            precision=lax.Precision.HIGHEST,
        )


def node_sums(ysum, lanes):
    total = jnp.zeros((16, NXY), jnp.float32)
    for iy in range(NODES):
        total = total + jnp.dot(
            ysum[iy], lanes[iy], preferred_element_type=jnp.float32, precision=lax.Precision.HIGHEST
        )
    return total


UP, DOWN, SIBLING, OTHER, RELAY, LOW_A, LOW_B, LOW_RELAY, HIGH_A, HIGH_B, HIGH_RELAY, NODE, TAIL = range(13)


def step_kernel(
    offs_hbm, sub_hbm, tomo_hbm, vol_hbm, res, rhs_ref,
    own, halo, tomo, lanes, volf, band_x, band_y, shifts, grads, lhs, win, ysum, fields, nodes, mine, above, sums, tail,
    offs, send, recv, local,
):
    bricks = lax.axis_size("brick")
    b = lax.axis_index("brick")
    s = lax.axis_index("scan")
    block = tomo_hbm.shape[0]
    has_above = b < bricks - 1
    has_below = b > 0
    odd = lax.rem(s, 2) == 1
    sibling = s + 1 - 2 * lax.rem(s, 2)
    other = lax.rem(s + 2, 4)

    def remote(kind, src, dst, brick, scan):
        return pltpu.make_async_remote_copy(
            src_ref=src,
            dst_ref=dst,
            send_sem=send.at[kind],
            recv_sem=recv.at[kind],
            device_id={"brick": brick, "scan": scan},
            device_id_type=pl.DeviceIdType.MESH,
        )

    def block_at(i):
        return tomo.at[pl.ds(RADIUS + block * i, block)]

    low_edge = tomo.at[pl.ds(0, RADIUS)]
    high_edge = tomo.at[pl.ds(RADIUS + E, RADIUS)]
    up = remote(UP, vol_hbm.at[0, pl.ds(E - HALO + 1, HALO - 1)], halo.at[0, pl.ds(1, HALO - 1)], b + 1, s)
    down = remote(DOWN, vol_hbm.at[0, pl.ds(0, HALO)], halo.at[1], b - 1, s)
    to_sibling = remote(SIBLING, tomo_hbm, block_at(s), b, sibling)
    to_other = remote(OTHER, tomo_hbm, block_at(s), b, other)
    relay = remote(RELAY, block_at(other), block_at(other), b, sibling)
    from_relay = remote(RELAY, block_at(lax.rem(sibling + 2, 4)), block_at(lax.rem(sibling + 2, 4)), b, sibling)
    from_sibling = remote(SIBLING, tomo_hbm, block_at(sibling), b, sibling)
    from_other = remote(OTHER, tomo_hbm, block_at(other), b, other)
    last_planes = tomo_hbm.at[pl.ds(block - RADIUS, RADIUS)]
    first_planes = tomo_hbm.at[pl.ds(0, RADIUS)]
    low_a = remote(LOW_A, last_planes, low_edge, b + 1, 3)
    low_b = remote(LOW_B, tomo.at[pl.ds(E, RADIUS)], low_edge, b + 1, 1)
    low_relay = remote(LOW_RELAY, low_edge, low_edge, b, sibling)
    high_a = remote(HIGH_A, first_planes, high_edge, b - 1, 0)
    high_b = remote(HIGH_B, tomo.at[pl.ds(RADIUS, RADIUS)], high_edge, b - 1, 2)
    high_relay = remote(HIGH_RELAY, high_edge, high_edge, b, sibling)
    node = remote(NODE, sub_hbm, above, b - 1, s)

    get_own = pltpu.make_async_copy(vol_hbm.at[0], own, local.at[0])
    get_tomo = pltpu.make_async_copy(tomo_hbm, block_at(s), local.at[1])
    get_offs = pltpu.make_async_copy(offs_hbm, offs, local.at[3])
    get_offs.start()
    get_sub = pltpu.make_async_copy(sub_hbm, mine, local.at[2])
    get_own.start()
    get_tomo.start()
    get_sub.start()

    barrier = pltpu.get_barrier_semaphore()

    def greet(brick, scan):
        pl.semaphore_signal(
            barrier, inc=1, device_id={"brick": brick, "scan": scan}, device_id_type=pl.DeviceIdType.MESH
        )

    greet(b, sibling)
    greet(b, other)

    @pl.when(has_above)
    def _():
        greet(b + 1, s)

    @pl.when(has_below)
    def _():
        greet(b - 1, s)

    pl.semaphore_wait(barrier, 2 + has_above.astype(jnp.int32) + has_below.astype(jnp.int32))

    @pl.when(has_above & (s == 3))
    def _():
        low_a.start()

    @pl.when(has_below & (s == 0))
    def _():
        high_a.start()

    to_other.start()
    to_sibling.start()

    @pl.when(has_below)
    def _():
        node.start()

    zeros_lo = jnp.zeros((YPAD, NXY), jnp.float32)
    zeros_hi = jnp.zeros((VROWS - YPAD - NXY, NXY), jnp.float32)

    def borders(z, _):
        volf[z, :YPAD] = zeros_lo
        volf[z, YPAD + NXY :] = zeros_hi
        return 0

    lax.fori_loop(0, VPLANES, borders, 0)
    nodes[...] = jnp.zeros_like(nodes)
    halo[0, 0] = jnp.zeros((NXY, NXY), jnp.bfloat16)
    get_sub.wait()
    for c in range(3):
        nodes[c : c + 1, : NODES * NODES] = mine[0, c]

    @pl.when(jnp.logical_not(has_below))
    def _():
        halo[0] = jnp.zeros((HALO, NXY, NXY), jnp.bfloat16)
        tomo[:RADIUS] = jnp.zeros((RADIUS, NXY, NXY), jnp.bfloat16)

    @pl.when(jnp.logical_not(has_above))
    def _():
        halo[1] = jnp.zeros((HALO, NXY, NXY), jnp.bfloat16)
        tomo[RADIUS + E :] = jnp.zeros((RADIUS, NXY, NXY), jnp.bfloat16)

    get_own.wait()

    def spread_own(z, _):
        volf[HALO + z, YPAD : YPAD + NXY] = own[z].astype(jnp.float32)
        return 0

    lax.fori_loop(0, E, spread_own, 0)

    def filter_block(i):
        filter_planes(band_x, band_y, tomo, grads, RADIUS + block * i, block)

    write_bands(band_x, band_y)
    get_tomo.wait()
    filter_block(s)

    from_other.wait_recv()
    relay.start()

    @pl.when(has_below & (lax.rem(b, 4) == 0))
    def _():
        down.start()

    @pl.when(has_above & (lax.rem(b, 4) == 3))
    def _():
        up.start()


    @pl.when(has_above & (s == 1))
    def _():
        low_b.start()

    @pl.when(has_below & (s == 2))
    def _():
        high_b.start()

    filter_block(other)

    @pl.when(has_below & (lax.rem(b, 4) != 0))
    def _():
        down.start()

    @pl.when(has_above & (lax.rem(b, 4) != 3))
    def _():
        up.start()

    from_sibling.wait_recv()
    filter_block(sibling)

    @pl.when(has_below & odd)
    def _():
        @pl.when(s == 3)
        def _():
            low_a.wait_recv()

        @pl.when(s == 1)
        def _():
            low_b.wait_recv()

        low_relay.start()

    @pl.when(has_above & jnp.logical_not(odd))
    def _():
        @pl.when(s == 0)
        def _():
            high_a.wait_recv()

        @pl.when(s == 2)
        def _():
            high_b.wait_recv()

        high_relay.start()

    get_offs.wait()
    write_shifts(offs, shifts)

    @pl.when(has_above)
    def _():
        node.wait_recv()
        for c in range(3):
            nodes[8 + c : 9 + c, : NODES * NODES] = above[0, c]

    node_fields(nodes, fields, lanes)
    from_relay.wait_recv()
    filter_block(lax.rem(sibling + 2, 4))

    @pl.when(has_below & jnp.logical_not(odd))
    def _():
        low_relay.wait_recv()

    @pl.when(has_above & odd)
    def _():
        high_relay.wait_recv()

    filter_planes(band_x, band_y, tomo, grads, 0, RADIUS)
    filter_planes(band_x, band_y, tomo, grads, RADIUS + E, RADIUS)
    filter_depth(grads)

    @pl.when(has_above)
    def _():
        down.wait_recv()

    @pl.when(has_below)
    def _():
        up.wait_recv()

    def spread_halo(z, _):
        volf[z, YPAD : YPAD + NXY] = halo[0, z].astype(jnp.float32)
        volf[HALO + E + z, YPAD : YPAD + NXY] = halo[1, z].astype(jnp.float32)
        return 0

    lax.fori_loop(0, HALO, spread_halo, 0)

    warp_layer(
        offs, shifts, fields, volf, tomo, grads, lhs, win, ysum, res
    )
    sums[...] = node_sums(ysum, lanes)
    to_above = remote(TAIL, sums.at[pl.ds(8, 8)], tail, b + 1, s)

    @pl.when(has_above)
    def _():
        to_above.start()

    to_other.wait_send()
    to_sibling.wait_send()
    relay.wait_send()

    @pl.when(has_above & (s == 3))
    def _():
        low_a.wait_send()

    @pl.when(has_above & (s == 1))
    def _():
        low_b.wait_send()

    @pl.when(has_below & (s == 0))
    def _():
        high_a.wait_send()

    @pl.when(has_below & (s == 2))
    def _():
        high_b.wait_send()

    @pl.when(has_below & odd)
    def _():
        low_relay.wait_send()

    @pl.when(has_above & jnp.logical_not(odd))
    def _():
        high_relay.wait_send()

    @pl.when(has_above)
    def _():
        up.wait_send()

    @pl.when(has_below)
    def _():
        down.wait_send()
        node.wait_send()

    @pl.when(jnp.logical_not(has_below))
    def _():
        tail[...] = jnp.zeros_like(tail)

    @pl.when(has_below)
    def _():
        to_above.wait_recv()

    final = sums[:8] + tail[...]
    for c in range(3):
        rhs_ref[0, c] = final[c : c + 1, : NODES * NODES]

    @pl.when(has_above)
    def _():
        to_above.wait_send()


def body(tomogram, deformed, subvoxel, offsets):
    tall = E + 2 * RADIUS
    smem = pl.BlockSpec(memory_space=pltpu.SMEM)
    vmem = pl.BlockSpec(memory_space=pltpu.VMEM)
    hbm = pl.BlockSpec(memory_space=pltpu.HBM)
    residual, node_rhs = pl.pallas_call(
        step_kernel,
        out_shape=(
            jax.ShapeDtypeStruct((E, NXY, NXY), jnp.bfloat16),
            jax.ShapeDtypeStruct(subvoxel.shape, jnp.float32),
        ),
        in_specs=[hbm, hbm, hbm, hbm],
        out_specs=(vmem, vmem),
        scratch_shapes=[
            pltpu.VMEM((E, NXY, NXY), jnp.bfloat16),
            pltpu.VMEM((2, HALO, NXY, NXY), jnp.bfloat16),
            pltpu.VMEM((tall, NXY, NXY), jnp.bfloat16),
            pltpu.VMEM((NODES, NXY, NXY), jnp.float32),
            pltpu.VMEM((VPLANES, VROWS, NXY), jnp.float32),
            pltpu.VMEM((NXY, 2 * NXY), jnp.bfloat16),
            pltpu.VMEM((2 * NXY, NXY), jnp.bfloat16),
            pltpu.VMEM((PER_ROW, PER_ROW * NXY, 2 * NXY), jnp.bfloat16),
            pltpu.VMEM((3, tall, NXY, NXY), jnp.float32),
            pltpu.VMEM((2, WPLANES * WIN, PER_ROW * NXY), jnp.bfloat16),
            pltpu.VMEM((2, WPLANES * WIN, NXY), jnp.float32),
            pltpu.VMEM((NODES, 16, NXY), jnp.float32),
            pltpu.VMEM((NODES, 16, NXY), jnp.float32),
            pltpu.VMEM((16, NXY), jnp.float32),
            pltpu.VMEM(subvoxel.shape, jnp.float32),
            pltpu.VMEM(subvoxel.shape, jnp.float32),
            pltpu.VMEM((16, NXY), jnp.float32),
            pltpu.VMEM((8, NXY), jnp.float32),
            pltpu.SMEM((3, 1, PER_ROW * PER_ROW), jnp.int32),
            pltpu.SemaphoreType.DMA((13,)),
            pltpu.SemaphoreType.DMA((13,)),
            pltpu.SemaphoreType.DMA((4,)),
        ],
        compiler_params=pltpu.CompilerParams(
            collective_id=0, has_side_effects=True, vmem_limit_bytes=50 << 20
        ),
    )(
        *[
            pltpu.with_memory_space_constraint(x, pltpu.HBM)
            for x in (offsets.transpose(1, 0, 2), subvoxel, tomogram, deformed)
        ],
    )
    return residual[None], node_rhs


def solution(mesh):
    return jax.shard_map(
        body,
        mesh=mesh,
        in_specs=(
            P(("brick", "scan"), None, None),
            P("scan", "brick", None, None),
            P("scan", None, "brick", None),
            P("scan", None, "brick"),
        ),
        out_specs=(P("scan", "brick", None, None), P("scan", None, "brick", None)),
        check_vma=False,
    )
```
